512 devices in a mesh: row: 32 (over y, x_hi, core), col: 16 (over z, x_lo).
Axes of the slice: x: 4 (x_hi: 2, x_lo: 2; x = x_hi * 2 + x_lo), y: 8, z: 8, core: 2. Of those that a mesh axis runs over, the one named last changes fastest.
Arguments:
- temps: bfloat16 [12, 64, 262144], P(None, None, ('row', 'col')), may hold values from -6 to 6
- sensors: int32 [12, 2048], replicated, may hold values from 0 to 262143
Outputs:
- corr: bfloat16 [2048, 262144], P('col', 'row')
The draws below stay inside these ranges and needn't reach their ends.
Inputs may be any that keep to these rules, and one draw needn't show every extreme that they name: `sensors`: each entry is a pixel index of its tier; candidates may repeat.
All inputs are finite; a program needn't handle non-finite values.
Results may differ from the reference program's by a relative error of at most 0.001.
Values may be sent and summed in bfloat16 or wider, within the bound.
No kernel may reach another device: no remote copies, remote signals or barrier semaphores. Data moves between devices by JAX's collectives and lax.ppermute only.
A program may use at most 64 MiB of HBM per device.

```python
import jax
import jax.numpy as jnp
from jax import lax

TIERS = 12
SNAP = 64
PIX_DEV = 512
PIX = 262144
SENS = 2048
N_ROW = 32
N_COL = 16


def with_ends(values, stream_key, low, top_value):
    longest = values.shape.index(max(values.shape))
    spots = []
    for shift in (0, 1):
        where = [jax.random.randint(jax.random.fold_in(stream_key, axis), (), 0, length) for axis, length in enumerate(values.shape)]
        where[longest] = (where[longest] + shift) % values.shape[longest]
        spots.append(tuple(where))
    return values.at[spots[0]].set(low).at[spots[1]].set(top_value)


def block_levels(own_key, dims, cuts, low, largest):
    def one(axis_at, parts):
        heights = jax.random.uniform(jax.random.fold_in(jax.random.fold_in(own_key, 6), axis_at), (parts,), jnp.float32, low / len(cuts), largest / len(cuts))
        return jnp.repeat(jnp.exp(heights), dims[axis_at] // parts).reshape((-1,) + (1,) * (len(dims) - axis_at - 1))

    loudness = one(*cuts[0])
    for cut in cuts[1:]:
        loudness = loudness * one(*cut)
    return loudness


def centred(own_key, shape, spread, reach, cuts=(), kind=jnp.bfloat16):
    array = jax.random.normal(own_key, shape, jnp.float32) * spread
    if len(cuts) > 0:
        array = block_levels(own_key, shape, cuts, -0.22, 0.18) * array
    return jnp.clip(array, min=-reach, max=reach).astype(kind)


def setup_inputs(seed: int = 0) -> dict:
    keys = jax.random.split(jax.random.key(seed), 3)
    return {
        "temps": centred(keys[0], (TIERS, SNAP, PIX), 1.0, 6.0, ((2, 512),)),
        "sensors": with_ends(jax.random.randint(keys[1], (TIERS, SENS), 0, PIX), jax.random.fold_in(keys[1], 1), 0, PIX - 1).astype(jnp.int32),
    }


def reference(temps, sensors):
    readings = jax.vmap(lambda fields, cols: jnp.take(fields, cols, axis=1))(temps, sensors)
    chosen = readings.astype(jnp.float32)
    block_width = PIX_DEV * N_COL
    scale_factor = 1.0 / jnp.sqrt(jnp.float32(TIERS * SNAP))

    def one_block(block_index):
        first_pixel = (block_index * block_width).astype(jnp.int32)
        fields = lax.dynamic_slice_in_dim(temps, first_pixel, block_width, 2).astype(jnp.float32)
        summed = jnp.einsum('tsc,tsp->cp', chosen, fields)
        return (summed * scale_factor).astype(jnp.bfloat16)
    blocks = lax.map(one_block, jnp.arange(N_ROW, dtype=jnp.int32))
    return jnp.transpose(blocks, (1, 0, 2)).reshape(SENS, PIX)
```

```python
import jax
import jax.numpy as jnp
from jax import lax
from jax.experimental import pallas as pl
from jax.experimental.pallas import tpu as pltpu
from jax.sharding import Mesh
from jax.sharding import PartitionSpec as P

AXES = ("y", "xh", "core", "z", "xl")
X = ("xh", "xl")
PLANE = ("y", "xh", "xl", "core")
VMEM = pl.BlockSpec(memory_space=pltpu.VMEM)


def ring(value, axis, shift):
    size = lax.axis_size(axis)
    return lax.ppermute(value, axis, [(i, (i + shift) % size) for i in range(size)])


def select_kernel(tiers, snaps, idx_ref, temps_ref, *rest):
    out_ref = rest[-1]
    rows, width = idx_ref.shape[0], temps_ref.shape[2]
    lanes = lax.broadcasted_iota(jnp.int32, (rows, width), 1)

    def one(tier):
        chosen = (lanes == idx_ref[:, tier : tier + 1]).astype(jnp.float32).astype(jnp.bfloat16)
        return lax.dot_general(
            chosen, temps_ref[tier], (((1,), (1,)), ((), ())), preferred_element_type=jnp.float32
        )

    for tier in range(0, tiers, 2):
        found = jnp.concatenate([one(tier), one(tier + 1)], axis=1)
        spot = slice(tier * snaps, (tier + 2) * snaps)
        if len(rest) > 1:
            found = found + rest[0][:, spot].astype(jnp.float32)
        out_ref[:, spot] = found.astype(jnp.bfloat16)


def select(idx, temps, *added):
    rows, tiers = idx.shape
    _, snaps, width = temps.shape
    depth, block = tiers * snaps, 256
    spec = pl.BlockSpec((block, depth), lambda i: (i, 0))
    return pl.pallas_call(
        lambda *refs: select_kernel(tiers, snaps, *refs),
        grid=(rows // block,),
        in_specs=[
            pl.BlockSpec((block, tiers), lambda i: (i, 0)),
            pl.BlockSpec(temps.shape, lambda i: (0, 0, 0)),
        ]
        + [spec] * len(added),
        out_specs=spec,
        out_shape=jax.ShapeDtypeStruct((rows, depth), jnp.bfloat16),
        cost_estimate=pl.CostEstimate(
            flops=2 * rows * depth * width, bytes_accessed=2 * rows * depth, transcendentals=0
        ),
        name="select",
    )(idx, temps, *added)


def body(temps, sensors):
    tiers, snaps, width = temps.shape
    depth = tiers * snaps
    n_y, n_x, n_core, n_z = (lax.axis_size(a) for a in ("y", X, "core", "z"))
    n_xl = lax.axis_size("xl")
    per_z = sensors.shape[1] // n_z
    piece = per_z // (n_y * n_x * n_core)
    core = lax.axis_index("core")

    gathered = lax.all_gather(temps, "z")

    other_temps = ring(temps, "core", 1)
    order = sensors.reshape(tiers, n_z, n_y, n_x, n_core, piece)
    order = lax.dynamic_index_in_dim(order, core, 4, keepdims=False)
    order = order.transpose(3, 1, 2, 4, 0).reshape(-1, tiers)
    first = lax.axis_index(AXES) * width
    stride = n_z * n_xl * width
    other_first = first + jnp.where(core == 0, stride, -stride)
    part = select(order - first, temps)
    part = select(order - other_first, other_temps, part)

    part = part.reshape(n_x, per_z * n_z // (n_x * n_core), depth)
    part = lax.all_to_all(part, X, 0, 0, tiled=True)
    part = part.astype(jnp.float32).sum(axis=0).astype(jnp.bfloat16)
    part = part.reshape(n_z * n_y, piece, depth)
    part = lax.all_to_all(part, ("z", "y"), 0, 0, tiled=True)
    part = part.astype(jnp.float32).sum(axis=0).astype(jnp.bfloat16)
    part = jnp.broadcast_to(part[None], (n_y * n_x * n_core, piece, depth))
    readings = lax.all_to_all(part, PLANE, 0, 0, tiled=True).reshape(per_z, depth)

    scale = 1.0 / jnp.sqrt(jnp.float32(depth))
    summed = jnp.einsum(
        "hck,zkp->hzcp",
        readings.reshape(n_xl, per_z // n_xl, depth),
        gathered.reshape(n_z, depth, width),
        preferred_element_type=jnp.float32,
    )
    corr = (summed * scale).astype(jnp.bfloat16)
    corr = lax.all_to_all(corr, "xl", 0, 0, tiled=True)
    return corr.transpose(2, 1, 0, 3).reshape(per_z // n_xl, -1)


def solution(mesh):
    torus = Mesh(mesh.devices.reshape(8, 2, 2, 8, 2), AXES)
    return jax.shard_map(
        body,
        mesh=torus,
        in_specs=(P(None, None, AXES), P()),
        out_specs=P(("z", "xl"), ("y", "xh", "core")),
        check_vma=False,
    )
```

```python
import functools
import math

import jax
import jax.numpy as jnp
from jax import lax
from jax.experimental import pallas as pl
from jax.experimental.pallas import tpu as pltpu
from jax.sharding import Mesh
from jax.sharding import PartitionSpec as P

AXES = ("y", "xh", "core", "z", "xl")
PLANE = ("y", "xh", "xl", "core")
SLOTS = 32
FIRST = 384
F32, BF16 = jnp.float32, jnp.bfloat16
PARAMS = pltpu.CompilerParams(vmem_limit_bytes=16 * 2**20)
NT = (((1,), (1,)), ((), ()))
VMEM = pl.BlockSpec(memory_space=pltpu.VMEM)
SMEM = pl.BlockSpec(memory_space=pltpu.SMEM)


def matmul(a, b, dims=(((1,), (0,)), ((), ()))):
    return lax.dot_general(a, b, dims, preferred_element_type=F32)


def ones(mask):
    return mask.astype(F32).astype(BF16)


def triangles(tiers, columns):
    upper = lax.broadcasted_iota(jnp.int32, (columns, columns), 0) < lax.broadcasted_iota(
        jnp.int32, (columns, columns), 1
    )
    lower = lax.broadcasted_iota(jnp.int32, (tiers, tiers), 0) > lax.broadcasted_iota(
        jnp.int32, (tiers, tiers), 1
    )
    return ones(upper), ones(lower)


def ranks(mask, upper, lower):
    mask = ones(mask)
    return matmul(mask, upper) + matmul(lower, mask).sum(axis=1, keepdims=True)


def compact_kernel(scalar_ref, sensors_ref, temps_ref, out_ref):
    n_z, half, _ = out_ref.shape
    tiers, _, width = temps_ref.shape
    slots, per_z = 2 * half, sensors_ref.shape[1] // n_z
    first, start = scalar_ref[0], scalar_ref[1]
    upper, lower = triangles(tiers, per_z)
    slot_ids = lax.broadcasted_iota(jnp.int32, (slots, per_z), 0)
    tier_ids = lax.broadcasted_iota(jnp.int32, (tiers, per_z), 0)
    spots = []
    for z in range(n_z):
        offset = sensors_ref[:, z * per_z : (z + 1) * per_z] - first
        mine = (offset >= 0) & (offset < width)
        slot = ranks(mine, upper, lower).astype(jnp.int32) - start
        slot = jnp.where(mine, slot, -1)
        spot = (offset + tier_ids * width + 1).astype(F32)
        found = jnp.zeros((slots, per_z), F32)
        for tier in range(tiers):
            row = slice(tier, tier + 1)
            found = found + jnp.where(slot[row] == slot_ids, spot[row], 0.0)
        spots.append(found.sum(axis=1, keepdims=True))
    spots = jnp.concatenate(spots, axis=0).astype(jnp.int32) - 1
    lanes = lax.broadcasted_iota(jnp.int32, (n_z * slots, width), 1)
    total = jnp.zeros((n_z * slots, temps_ref.shape[1]), F32)
    for tier in range(tiers):
        total = total + matmul(ones(spots - tier * width == lanes), temps_ref[tier], NT)
    for z in range(n_z):
        low = z * slots
        out_ref[z] = jnp.concatenate(
            [total[low : low + half], total[low + half : low + slots]], axis=1
        ).astype(BF16)


def compact(scalars, sensors, temps, n_z):
    return pl.pallas_call(
        compact_kernel,
        in_specs=[SMEM, VMEM, VMEM],
        out_specs=VMEM,
        out_shape=jax.ShapeDtypeStruct((n_z, SLOTS // 2, 2 * temps.shape[1]), BF16),
        compiler_params=PARAMS,
        name="compact",
    )(scalars, sensors, temps)


def expand_kernel(width, scalar_ref, sensors_ref, lists_ref, out_ref):
    n_z, half, wide = lists_ref.shape
    snaps = wide // 2
    tiers = sensors_ref.shape[0]
    per_z = out_ref.shape[0]
    first, start, stride = scalar_ref[0], scalar_ref[1], 2 * width
    own = pl.multiple_of(scalar_ref[2], per_z)
    upper, lower = triangles(tiers, per_z)
    offset = sensors_ref[:, pl.ds(own, per_z)] - first
    spot = jnp.full((tiers, per_z), -1, jnp.int32)
    for z in range(n_z):
        there = (offset >= z * stride) & (offset < z * stride + width)
        slot = ranks(there, upper, lower).astype(jnp.int32) - start
        code = jnp.where(slot < half, slot + z * half, slot + (n_z - 1 + z) * half)
        spot = jnp.where(there & (slot >= 0) & (slot < 2 * half), code, spot)
    eye = lax.broadcasted_iota(jnp.int32, (tiers, tiers), 0) == lax.broadcasted_iota(
        jnp.int32, (tiers, tiers), 1
    )
    column = lax.dot_general(
        spot.astype(F32).astype(BF16), ones(eye), (((0,), (0,)), ((), ())), preferred_element_type=F32
    ).astype(jnp.int32)
    lists = lists_ref[...].reshape(n_z * half, wide)
    lists = jnp.concatenate([lists[:, :snaps], lists[:, snaps:]], axis=0)
    lanes = lax.broadcasted_iota(jnp.int32, (per_z, 2 * n_z * half), 1)
    for tier in range(0, tiers, 2):
        pair = [matmul(ones(lanes == column[:, t : t + 1]), lists) for t in (tier, tier + 1)]
        out_ref[:, tier * snaps : (tier + 2) * snaps] = jnp.concatenate(pair, axis=1).astype(BF16)


def expand(scalars, sensors, lists, width):
    n_z, _, wide = lists.shape
    tiers, count = sensors.shape
    return pl.pallas_call(
        functools.partial(expand_kernel, width),
        in_specs=[SMEM, VMEM, VMEM],
        out_specs=VMEM,
        out_shape=jax.ShapeDtypeStruct((count // n_z, tiers * wide // 2), BF16),
        compiler_params=PARAMS,
        name="expand",
    )(scalars, sensors, lists)


def longest_kernel(n_z, devices, width, sensors_ref, out_ref):
    tiers, count = sensors_ref.shape
    per_z, low = count // n_z, 16
    high_ids = lax.broadcasted_iota(jnp.int32, (devices // low, per_z), 0)
    low_ids = lax.broadcasted_iota(jnp.int32, (low, per_z), 0)
    most = jnp.zeros((devices // low, low), F32)
    for z in range(n_z):
        owner = sensors_ref[:, z * per_z : (z + 1) * per_z] // width
        total = jnp.zeros_like(most)
        for tier in range(tiers):
            row = owner[tier : tier + 1]
            total = total + matmul(ones(row // low == high_ids), ones(row % low == low_ids), NT)
        most = jnp.maximum(most, total)
    out_ref[0, 0] = jnp.max(most).astype(jnp.int32)


def longest(sensors, n_z, devices, width):
    return pl.pallas_call(
        functools.partial(longest_kernel, n_z, devices, width),
        in_specs=[VMEM],
        out_specs=SMEM,
        out_shape=jax.ShapeDtypeStruct((1, 1), jnp.int32),
        compiler_params=PARAMS,
        cost_estimate=pl.CostEstimate(
            flops=2 * sensors.size * devices, bytes_accessed=4 * sensors.size, transcendentals=0
        ),
        name="longest",
    )(sensors)[0, 0]


def correlate_kernel(scale, scalar_ref, readings_ref, pixels_ref, *rest):
    summed = matmul(readings_ref[...], pixels_ref[...])
    rest[-1][...] = (summed * scale).astype(BF16)


def block_columns(rows, stride, skipped, width):
    def place_of(z, h):
        return 0, pl.multiple_of((2 * z + h[1]) * stride + skipped, 128)

    return pl.BlockSpec((pl.Element(rows), pl.Element(width)), place_of)


def correlate(half, readings, pixels, out_spec, out_shape, *whole):
    n_z, depth, width = pixels.shape
    rows = readings.shape[0] // 2
    return pl.pallas_call(
        functools.partial(correlate_kernel, 1.0 / math.sqrt(depth)),
        grid_spec=pltpu.PrefetchScalarGridSpec(
            num_scalar_prefetch=1,
            grid=(n_z,),
            in_specs=[
                pl.BlockSpec((rows, depth), lambda z, h: (h[0], 0)),
                pl.BlockSpec((None, depth, width), lambda z, h: (z, 0, 0)),
            ]
            + [pl.BlockSpec(memory_space=pl.ANY)] * len(whole),
            out_specs=out_spec,
        ),
        out_shape=jax.ShapeDtypeStruct(out_shape, BF16),
        input_output_aliases={3: 0} if whole else {},
        cost_estimate=pl.CostEstimate(
            flops=2 * rows * depth * width * n_z, bytes_accessed=pixels.size * 2, transcendentals=0
        ),
        compiler_params=pltpu.CompilerParams(vmem_limit_bytes=59 * 2**20),
        name="correlate",
    )(half, readings, pixels, *whole)


def place_kernel(scalar_ref, block_ref, whole_ref, out_ref):
    out_ref[...] = block_ref[...]


def place(side, blocks, out_spec, whole):
    n_z, rows, width = blocks.shape
    return pl.pallas_call(
        place_kernel,
        grid_spec=pltpu.PrefetchScalarGridSpec(
            num_scalar_prefetch=1,
            grid=(n_z,),
            in_specs=[
                pl.BlockSpec((None, rows, width), lambda z, h: (z, 0, 0)),
                pl.BlockSpec(memory_space=pl.ANY),
            ],
            out_specs=out_spec,
        ),
        out_shape=jax.ShapeDtypeStruct(whole.shape, BF16),
        input_output_aliases={2: 0},
        compiler_params=PARAMS,
        name="place",
    )(side, blocks, whole)


def body(temps, sensors):
    tiers, snaps, width = temps.shape
    depth = tiers * snaps
    n_z, n_plane, devices = (lax.axis_size(a) for a in ("z", PLANE, AXES))
    per_z = sensors.shape[1] // n_z
    piece = per_z // n_plane
    rows = per_z // 2
    z, xl = lax.axis_index("z"), lax.axis_index("xl")

    spans = [(0, FIRST), (FIRST, width - FIRST)]
    gathered = [
        lax.all_gather(lax.slice_in_dim(temps, low, low + size, axis=2), "z").reshape(
            n_z, depth, size
        )
        for low, size in spans
    ]

    first = lax.axis_index(AXES) * width
    column_first = first - z * lax.axis_size("xl") * width

    def one_round(number):
        start = number * SLOTS
        lists = compact(jnp.stack([first, start]), sensors, temps, n_z)
        lists = lax.all_to_all(lists, "z", 0, 0, tiled=True)
        part = expand(jnp.stack([column_first, start, z * per_z]), sensors, lists, width)
        seen, part = lax.optimization_barrier((sensors, part))
        part = lax.all_to_all(part.reshape(n_plane, piece, depth), PLANE, 0, 0, tiled=True)
        part = part.astype(F32).sum(axis=0).astype(BF16)
        part = jnp.broadcast_to(part[None], (n_plane, piece, depth))
        return seen, lax.all_to_all(part, PLANE, 0, 0, tiled=True).reshape(per_z, depth)

    seen, readings = one_round(jnp.int32(0))
    rounds = pl.cdiv(longest(seen, n_z, devices, width), SLOTS)
    _, readings = lax.while_loop(
        lambda state: state[0] < rounds,
        lambda state: (state[0] + 1, state[1] + one_round(state[0])[1]),
        (jnp.int32(1), readings),
    )

    theirs, mine = jnp.stack([1 - xl, xl]), jnp.stack([xl, xl])
    there = jnp.stack([xl, 1 - xl])
    whole, shape = (), (rows, 2 * n_z * width)
    for pixels, (low, size) in zip(gathered, spans, strict=True):
        pixels, *whole = lax.optimization_barrier((pixels, *whole))
        sent = correlate(
            theirs,
            readings,
            pixels,
            pl.BlockSpec((None, rows, size), lambda z, h: (z, 0, 0)),
            (n_z, rows, size),
        )
        arrived = lax.ppermute(sent, "xl", [(0, 1), (1, 0)])
        spec = block_columns(rows, width, low, size)
        own = correlate(mine, readings, pixels, spec, shape, *whole)
        whole = (place(there, arrived, spec, own),)
    return whole[0]


def solution(mesh):
    torus = Mesh(mesh.devices.reshape(8, 2, 2, 8, 2), AXES)
    return jax.shard_map(
        body,
        mesh=torus,
        in_specs=(P(None, None, AXES), P()),
        out_specs=P(("z", "xl"), ("y", "xh", "core")),
        check_vma=False,
    )
```

```python
import functools
import math

import jax
import jax.numpy as jnp
from jax import lax
from jax.experimental import pallas as pl
from jax.experimental.pallas import tpu as pltpu
from jax.sharding import Mesh
from jax.sharding import PartitionSpec as P

AXES = ("y", "xh", "core", "z", "xl")
PLANE = ("y", "xh", "xl", "core")
SLOTS = 32
F32, BF16 = jnp.float32, jnp.bfloat16
PARAMS = pltpu.CompilerParams(vmem_limit_bytes=16 * 2**20)
NT = (((1,), (1,)), ((), ()))
VMEM = pl.BlockSpec(memory_space=pltpu.VMEM)
SMEM = pl.BlockSpec(memory_space=pltpu.SMEM)
HBM = pl.BlockSpec(memory_space=pl.ANY)


def matmul(a, b, dims=(((1,), (0,)), ((), ()))):
    return lax.dot_general(a, b, dims, preferred_element_type=F32)


def ones(mask):
    return mask.astype(F32).astype(BF16)


def triangles(tiers, columns):
    upper = lax.broadcasted_iota(jnp.int32, (columns, columns), 0) < lax.broadcasted_iota(
        jnp.int32, (columns, columns), 1
    )
    lower = lax.broadcasted_iota(jnp.int32, (tiers, tiers), 0) > lax.broadcasted_iota(
        jnp.int32, (tiers, tiers), 1
    )
    return ones(upper), ones(lower)


def ranks(mask, upper, lower):
    mask = ones(mask)
    return matmul(mask, upper) + matmul(lower, mask).sum(axis=1, keepdims=True)


def compact_kernel(scalar_ref, sensors_ref, temps_ref, out_ref):
    n_z, half, _ = out_ref.shape
    tiers, _, width = temps_ref.shape
    slots, per_z = 2 * half, sensors_ref.shape[1] // n_z
    first, start = scalar_ref[0], scalar_ref[1]
    upper, lower = triangles(tiers, per_z)
    slot_ids = lax.broadcasted_iota(jnp.int32, (slots, per_z), 0)
    tier_ids = lax.broadcasted_iota(jnp.int32, (tiers, per_z), 0)
    spots = []
    for z in range(n_z):
        offset = sensors_ref[:, z * per_z : (z + 1) * per_z] - first
        mine = (offset >= 0) & (offset < width)
        slot = ranks(mine, upper, lower).astype(jnp.int32) - start
        slot = jnp.where(mine, slot, -1)
        spot = (offset + tier_ids * width + 1).astype(F32)
        found = jnp.zeros((slots, per_z), F32)
        for tier in range(tiers):
            row = slice(tier, tier + 1)
            found = found + jnp.where(slot[row] == slot_ids, spot[row], 0.0)
        spots.append(found.sum(axis=1, keepdims=True))
    spots = jnp.concatenate(spots, axis=0).astype(jnp.int32) - 1
    lanes = lax.broadcasted_iota(jnp.int32, (n_z * slots, width), 1)
    total = jnp.zeros((n_z * slots, temps_ref.shape[1]), F32)
    for tier in range(tiers):
        total = total + matmul(ones(spots - tier * width == lanes), temps_ref[tier], NT)
    for z in range(n_z):
        low = z * slots
        out_ref[z] = jnp.concatenate(
            [total[low : low + half], total[low + half : low + slots]], axis=1
        ).astype(BF16)


def compact(scalars, sensors, temps, n_z):
    return pl.pallas_call(
        compact_kernel,
        in_specs=[SMEM, VMEM, VMEM],
        out_specs=VMEM,
        out_shape=jax.ShapeDtypeStruct((n_z, SLOTS // 2, 2 * temps.shape[1]), BF16),
        compiler_params=PARAMS,
        name="compact",
    )(scalars, sensors, temps)


def expand_kernel(width, scalar_ref, sensors_ref, lists_ref, out_ref):
    n_z, half, wide = lists_ref.shape
    snaps = wide // 2
    tiers = sensors_ref.shape[0]
    per_z = out_ref.shape[0]
    first, start, stride = scalar_ref[0], scalar_ref[1], 2 * width
    own = pl.multiple_of(scalar_ref[2], per_z)
    upper, lower = triangles(tiers, per_z)
    offset = sensors_ref[:, pl.ds(own, per_z)] - first
    spot = jnp.full((tiers, per_z), -1, jnp.int32)
    for z in range(n_z):
        there = (offset >= z * stride) & (offset < z * stride + width)
        slot = ranks(there, upper, lower).astype(jnp.int32) - start
        code = jnp.where(slot < half, slot + z * half, slot + (n_z - 1 + z) * half)
        spot = jnp.where(there & (slot >= 0) & (slot < 2 * half), code, spot)
    eye = lax.broadcasted_iota(jnp.int32, (tiers, tiers), 0) == lax.broadcasted_iota(
        jnp.int32, (tiers, tiers), 1
    )
    column = lax.dot_general(
        spot.astype(F32).astype(BF16), ones(eye), (((0,), (0,)), ((), ())), preferred_element_type=F32
    ).astype(jnp.int32)
    lists = lists_ref[...].reshape(n_z * half, wide)
    lists = jnp.concatenate([lists[:, :snaps], lists[:, snaps:]], axis=0)
    lanes = lax.broadcasted_iota(jnp.int32, (per_z, 2 * n_z * half), 1)
    for tier in range(0, tiers, 2):
        pair = [matmul(ones(lanes == column[:, t : t + 1]), lists) for t in (tier, tier + 1)]
        out_ref[:, tier * snaps : (tier + 2) * snaps] = jnp.concatenate(pair, axis=1).astype(BF16)


def expand(scalars, sensors, lists, width):
    n_z, _, wide = lists.shape
    tiers, count = sensors.shape
    return pl.pallas_call(
        functools.partial(expand_kernel, width),
        in_specs=[SMEM, VMEM, VMEM],
        out_specs=VMEM,
        out_shape=jax.ShapeDtypeStruct((count // n_z, tiers * wide // 2), BF16),
        compiler_params=PARAMS,
        name="expand",
    )(scalars, sensors, lists)


def longest_kernel(n_z, devices, width, sensors_ref, out_ref):
    tiers, count = sensors_ref.shape
    per_z, low = count // n_z, 16
    high_ids = lax.broadcasted_iota(jnp.int32, (devices // low, per_z), 0)
    low_ids = lax.broadcasted_iota(jnp.int32, (low, per_z), 0)
    most = jnp.zeros((devices // low, low), F32)
    for z in range(n_z):
        owner = sensors_ref[:, z * per_z : (z + 1) * per_z] // width
        total = jnp.zeros_like(most)
        for tier in range(tiers):
            row = owner[tier : tier + 1]
            total = total + matmul(ones(row // low == high_ids), ones(row % low == low_ids), NT)
        most = jnp.maximum(most, total)
    out_ref[0, 0] = jnp.max(most).astype(jnp.int32)


def longest(sensors, n_z, devices, width):
    return pl.pallas_call(
        functools.partial(longest_kernel, n_z, devices, width),
        in_specs=[VMEM],
        out_specs=SMEM,
        out_shape=jax.ShapeDtypeStruct((1, 1), jnp.int32),
        compiler_params=PARAMS,
        cost_estimate=pl.CostEstimate(
            flops=2 * sensors.size * devices, bytes_accessed=4 * sensors.size, transcendentals=0
        ),
        name="longest",
    )(sensors)[0, 0]


def correlate_kernel(scale, scalar_ref, readings_ref, pixels_ref, out_ref, taken, done, *rest):
    n_z, _, width = taken.shape
    rows = readings_ref.shape[0] // 2
    loads = [pltpu.make_async_copy(pixels_ref.at[z], taken.at[z], done.at[z]) for z in range(n_z)]
    for load in loads:
        load.start()
    readings = readings_ref[pl.ds(pl.multiple_of(scalar_ref[0] * rows, rows), rows)]
    stores = []
    for z in range(n_z):
        loads[z].wait()
        summed = (matmul(readings, taken[z]) * scale).astype(BF16)
        if not rest:
            out_ref[z] = summed
            continue
        made, stored = rest
        made[z] = summed
        spot = pl.multiple_of((2 * z + scalar_ref[0]) * width, width)
        stores.append(
            pltpu.make_async_copy(made.at[z], out_ref.at[:, pl.ds(spot, width)], stored.at[z])
        )
        stores[-1].start()
    for store in stores:
        store.wait()


def correlate(half, readings, pixels, placed):
    n_z, depth, width = pixels.shape
    rows = readings.shape[0] // 2
    blocks = (n_z, rows, width)
    scratch = [pltpu.VMEM(pixels.shape, BF16), pltpu.SemaphoreType.DMA((n_z,))]
    if placed:
        scratch += [pltpu.VMEM(blocks, BF16), pltpu.SemaphoreType.DMA((n_z,))]
    return pl.pallas_call(
        functools.partial(correlate_kernel, 1.0 / math.sqrt(depth)),
        in_specs=[SMEM, VMEM, HBM],
        out_specs=HBM if placed else VMEM,
        out_shape=jax.ShapeDtypeStruct((rows, 2 * n_z * width) if placed else blocks, BF16),
        scratch_shapes=scratch,
        cost_estimate=pl.CostEstimate(
            flops=2 * rows * depth * width * n_z, bytes_accessed=pixels.size * 2, transcendentals=0
        ),
        compiler_params=pltpu.CompilerParams(vmem_limit_bytes=58 * 2**20),
        name="correlate",
    )(half, readings, pixels)


def place_kernel(scalar_ref, blocks_ref, whole_ref, out_ref, done):
    n_z, _, width = blocks_ref.shape
    stores = []
    for z in range(n_z):
        spot = pl.multiple_of((2 * z + scalar_ref[0]) * width, width)
        stores.append(
            pltpu.make_async_copy(blocks_ref.at[z], out_ref.at[:, pl.ds(spot, width)], done.at[z])
        )
        stores[-1].start()
    for store in stores:
        store.wait()


def place(side, blocks, whole):
    return pl.pallas_call(
        place_kernel,
        in_specs=[SMEM, HBM, HBM],
        out_specs=HBM,
        out_shape=jax.ShapeDtypeStruct(whole.shape, BF16),
        scratch_shapes=[pltpu.SemaphoreType.DMA((blocks.shape[0],))],
        input_output_aliases={2: 0},
        compiler_params=PARAMS,
        name="place",
    )(side, blocks, whole)


def body(temps, sensors):
    tiers, snaps, width = temps.shape
    depth = tiers * snaps
    n_z, n_plane, devices = (lax.axis_size(a) for a in ("z", PLANE, AXES))
    per_z = sensors.shape[1] // n_z
    piece = per_z // n_plane
    z, xl = lax.axis_index("z"), lax.axis_index("xl")

    gathered = lax.all_gather(temps, "z").reshape(n_z, depth, width)

    first = lax.axis_index(AXES) * width
    column_first = first - z * lax.axis_size("xl") * width

    def one_round(number):
        start = number * SLOTS
        lists = compact(jnp.stack([first, start]), sensors, temps, n_z)
        lists = lax.all_to_all(lists, "z", 0, 0, tiled=True)
        part = expand(jnp.stack([column_first, start, z * per_z]), sensors, lists, width)
        seen, part = lax.optimization_barrier((sensors, part))
        part = lax.all_to_all(part.reshape(n_plane, piece, depth), PLANE, 0, 0, tiled=True)
        part = part.astype(F32).sum(axis=0).astype(BF16)
        part = jnp.broadcast_to(part[None], (n_plane, piece, depth))
        return seen, lax.all_to_all(part, PLANE, 0, 0, tiled=True).reshape(per_z, depth)

    seen, readings = one_round(jnp.int32(0))
    rounds = pl.cdiv(longest(seen, n_z, devices, width), SLOTS)
    _, readings = lax.while_loop(
        lambda state: state[0] < rounds,
        lambda state: (state[0] + 1, state[1] + one_round(state[0])[1]),
        (jnp.int32(1), readings),
    )

    own, other = jnp.stack([xl]), jnp.stack([1 - xl])
    sent = correlate(other, readings, gathered, False)
    arrived = lax.ppermute(sent, "xl", [(0, 1), (1, 0)])
    whole = correlate(own, readings, gathered, True)
    return place(other, arrived, whole)


def solution(mesh):
    torus = Mesh(mesh.devices.reshape(8, 2, 2, 8, 2), AXES)
    return jax.shard_map(
        body,
        mesh=torus,
        in_specs=(P(None, None, AXES), P()),
        out_specs=P(("z", "xl"), ("y", "xh", "core")),
        check_vma=False,
    )
```

```python
import functools
import math

import jax
import jax.numpy as jnp
from jax import lax
from jax.experimental import pallas as pl
from jax.experimental.pallas import tpu as pltpu
from jax.sharding import Mesh
from jax.sharding import PartitionSpec as P

AXES = ("y", "xh", "core", "z", "xl")
PLANE = ("y", "xh", "xl", "core")
SLOTS = 32
F32, BF16 = jnp.float32, jnp.bfloat16
PARAMS = pltpu.CompilerParams(vmem_limit_bytes=16 * 2**20)
NT = (((1,), (1,)), ((), ()))
VMEM = pl.BlockSpec(memory_space=pltpu.VMEM)
SMEM = pl.BlockSpec(memory_space=pltpu.SMEM)
HBM = pl.BlockSpec(memory_space=pl.ANY)


def matmul(a, b, dims=(((1,), (0,)), ((), ()))):
    return lax.dot_general(a, b, dims, preferred_element_type=F32)


def ones(mask):
    return mask.astype(F32).astype(BF16)


def triangles(tiers, columns):
    upper = lax.broadcasted_iota(jnp.int32, (columns, columns), 0) < lax.broadcasted_iota(
        jnp.int32, (columns, columns), 1
    )
    lower = lax.broadcasted_iota(jnp.int32, (tiers, tiers), 0) > lax.broadcasted_iota(
        jnp.int32, (tiers, tiers), 1
    )
    return ones(upper), ones(lower)


def ranks(mask, upper, lower):
    mask = ones(mask)
    return matmul(mask, upper) + matmul(lower, mask).sum(axis=1, keepdims=True)


def compact_kernel(scalar_ref, sensors_ref, temps_ref, out_ref):
    n_z, half, _ = out_ref.shape
    tiers, _, width = temps_ref.shape
    slots, per_z = 2 * half, sensors_ref.shape[1] // n_z
    first, start = scalar_ref[0], scalar_ref[1]
    upper, lower = triangles(tiers, per_z)
    slot_ids = lax.broadcasted_iota(jnp.int32, (slots, per_z), 0)
    tier_ids = lax.broadcasted_iota(jnp.int32, (tiers, per_z), 0)
    spots = []
    for z in range(n_z):
        offset = sensors_ref[:, z * per_z : (z + 1) * per_z] - first
        mine = (offset >= 0) & (offset < width)
        slot = ranks(mine, upper, lower).astype(jnp.int32) - start
        slot = jnp.where(mine, slot, -1)
        spot = (offset + tier_ids * width + 1).astype(F32)
        found = jnp.zeros((slots, per_z), F32)
        for tier in range(tiers):
            row = slice(tier, tier + 1)
            found = found + jnp.where(slot[row] == slot_ids, spot[row], 0.0)
        spots.append(found.sum(axis=1, keepdims=True))
    spots = jnp.concatenate(spots, axis=0).astype(jnp.int32) - 1
    lanes = lax.broadcasted_iota(jnp.int32, (n_z * slots, width), 1)
    total = jnp.zeros((n_z * slots, temps_ref.shape[1]), F32)
    for tier in range(tiers):
        total = total + matmul(ones(spots - tier * width == lanes), temps_ref[tier], NT)
    for z in range(n_z):
        low = z * slots
        out_ref[z] = jnp.concatenate(
            [total[low : low + half], total[low + half : low + slots]], axis=1
        ).astype(BF16)


def compact(scalars, sensors, temps, n_z):
    return pl.pallas_call(
        compact_kernel,
        in_specs=[SMEM, VMEM, VMEM],
        out_specs=VMEM,
        out_shape=jax.ShapeDtypeStruct((n_z, SLOTS // 2, 2 * temps.shape[1]), BF16),
        compiler_params=PARAMS,
        name="compact",
    )(scalars, sensors, temps)


def expand_kernel(width, scalar_ref, sensors_ref, lists_ref, out_ref):
    n_z, half, wide = lists_ref.shape
    snaps = wide // 2
    tiers = sensors_ref.shape[0]
    per_z = out_ref.shape[0]
    first, start, stride = scalar_ref[0], scalar_ref[1], 2 * width
    own = pl.multiple_of(scalar_ref[2], per_z)
    upper, lower = triangles(tiers, per_z)
    offset = sensors_ref[:, pl.ds(own, per_z)] - first
    spot = jnp.full((tiers, per_z), -1, jnp.int32)
    for z in range(n_z):
        there = (offset >= z * stride) & (offset < z * stride + width)
        slot = ranks(there, upper, lower).astype(jnp.int32) - start
        code = jnp.where(slot < half, slot + z * half, slot + (n_z - 1 + z) * half)
        spot = jnp.where(there & (slot >= 0) & (slot < 2 * half), code, spot)
    eye = lax.broadcasted_iota(jnp.int32, (tiers, tiers), 0) == lax.broadcasted_iota(
        jnp.int32, (tiers, tiers), 1
    )
    column = lax.dot_general(
        spot.astype(F32).astype(BF16), ones(eye), (((0,), (0,)), ((), ())), preferred_element_type=F32
    ).astype(jnp.int32)
    lists = lists_ref[...].reshape(n_z * half, wide)
    lists = jnp.concatenate([lists[:, :snaps], lists[:, snaps:]], axis=0)
    lanes = lax.broadcasted_iota(jnp.int32, (per_z, 2 * n_z * half), 1)
    for tier in range(0, tiers, 2):
        pair = [matmul(ones(lanes == column[:, t : t + 1]), lists) for t in (tier, tier + 1)]
        out_ref[:, tier * snaps : (tier + 2) * snaps] = jnp.concatenate(pair, axis=1).astype(BF16)


def expand(scalars, sensors, lists, width):
    n_z, _, wide = lists.shape
    tiers, count = sensors.shape
    return pl.pallas_call(
        functools.partial(expand_kernel, width),
        in_specs=[SMEM, VMEM, VMEM],
        out_specs=VMEM,
        out_shape=jax.ShapeDtypeStruct((count // n_z, tiers * wide // 2), BF16),
        compiler_params=PARAMS,
        name="expand",
    )(scalars, sensors, lists)


def longest_kernel(n_z, devices, width, sensors_ref, out_ref):
    tiers, count = sensors_ref.shape
    per_z, low = count // n_z, 16
    high_ids = lax.broadcasted_iota(jnp.int32, (devices // low, per_z), 0)
    low_ids = lax.broadcasted_iota(jnp.int32, (low, per_z), 0)
    most = jnp.zeros((devices // low, low), F32)
    for z in range(n_z):
        owner = sensors_ref[:, z * per_z : (z + 1) * per_z] // width
        total = jnp.zeros_like(most)
        for tier in range(tiers):
            row = owner[tier : tier + 1]
            total = total + matmul(ones(row // low == high_ids), ones(row % low == low_ids), NT)
        most = jnp.maximum(most, total)
    out_ref[0, 0] = jnp.max(most).astype(jnp.int32)


def longest(sensors, n_z, devices, width):
    return pl.pallas_call(
        functools.partial(longest_kernel, n_z, devices, width),
        in_specs=[VMEM],
        out_specs=SMEM,
        out_shape=jax.ShapeDtypeStruct((1, 1), jnp.int32),
        compiler_params=PARAMS,
        cost_estimate=pl.CostEstimate(
            flops=2 * sensors.size * devices, bytes_accessed=4 * sensors.size, transcendentals=0
        ),
        name="longest",
    )(sensors)[0, 0]


def correlation(scale, readings, block):
    depth = readings.shape[1] // len(block)
    parts = [
        matmul(readings[:, i * depth : (i + 1) * depth], part[...]) for i, part in enumerate(block)
    ]
    return (sum(parts[1:], parts[0]) * scale).astype(BF16)


def half_of(readings_ref, side):
    rows = readings_ref.shape[0] // 2
    return readings_ref[pl.ds(pl.multiple_of(side * rows, rows), rows)]


def grouped(refs, sizes):
    refs = iter(refs)
    return [[next(refs) for _ in range(size)] for size in sizes]


def send_kernel(scale, sizes, scalar_ref, readings_ref, *rest):
    readings = half_of(readings_ref, 1 - scalar_ref[1])
    for spot, block in enumerate(grouped(rest[:-1], sizes)):
        rest[-1][spot] = correlation(scale, readings, block)


def keep_kernel(scale, n_z, shifts, sizes, scalar_ref, readings_ref, *rest):
    *refs, out_ref, made, stored = rest
    readings = half_of(readings_ref, scalar_ref[1])
    stores = []
    for spot, block in enumerate(grouped(refs, sizes)):
        made[spot] = correlation(scale, readings, block)
        stores.append(
            pltpu.make_async_copy(
                made.at[spot], columns(out_ref, n_z, shifts[spot], scalar_ref, 0), stored.at[spot]
            )
        )
        stores[-1].start()
    for store in stores:
        store.wait()


def columns(out_ref, n_z, shift, scalar_ref, other):
    width = out_ref.shape[1] // (2 * n_z)
    side = 1 - scalar_ref[1] if other else scalar_ref[1]
    spot = (2 * lax.rem(scalar_ref[0] + shift + n_z, n_z) + side) * width
    return out_ref.at[:, pl.ds(pl.multiple_of(spot, width), width)]


def place_kernel(n_z, shifts, scalar_ref, *rest):
    *pieces, _, out_ref, done = rest
    stores = []
    for piece in pieces:
        for i in range(piece.shape[0]):
            spot = len(stores)
            stores.append(
                pltpu.make_async_copy(
                    piece.at[i], columns(out_ref, n_z, shifts[spot], scalar_ref, 1), done.at[spot]
                )
            )
            stores[-1].start()
    for store in stores:
        store.wait()


def cost(blocks, rows):
    pixels = sum(part.size for block in blocks for part in block)
    return pl.CostEstimate(flops=2 * rows * pixels, bytes_accessed=2 * pixels, transcendentals=0)


def send(here, readings, blocks):
    rows, depth = readings.shape[0] // 2, readings.shape[1]
    parts = [part for block in blocks for part in block]
    return pl.pallas_call(
        functools.partial(send_kernel, 1.0 / math.sqrt(depth), [len(block) for block in blocks]),
        in_specs=[SMEM, VMEM] + [VMEM] * len(parts),
        out_specs=VMEM,
        out_shape=jax.ShapeDtypeStruct((len(blocks), rows, parts[0].shape[1]), BF16),
        cost_estimate=cost(blocks, rows),
        compiler_params=PARAMS,
        name="send",
    )(here, readings, *parts)


def keep(here, readings, blocks, shifts):
    rows, depth = readings.shape[0] // 2, readings.shape[1]
    parts = [part for block in blocks for part in block]
    count, width = len(blocks), parts[0].shape[1]
    return pl.pallas_call(
        functools.partial(
            keep_kernel, 1.0 / math.sqrt(depth), count, shifts, [len(block) for block in blocks]
        ),
        in_specs=[SMEM, VMEM] + [VMEM] * len(parts),
        out_specs=HBM,
        out_shape=jax.ShapeDtypeStruct((rows, 2 * count * width), BF16),
        scratch_shapes=[pltpu.VMEM((count, rows, width), BF16), pltpu.SemaphoreType.DMA((count,))],
        cost_estimate=cost(blocks, rows),
        compiler_params=PARAMS,
        name="keep",
    )(here, readings, *parts)


def place(here, pieces, shifts, whole):
    return pl.pallas_call(
        functools.partial(place_kernel, len(shifts), shifts),
        in_specs=[SMEM] + [HBM] * (len(pieces) + 1),
        out_specs=HBM,
        out_shape=jax.ShapeDtypeStruct(whole.shape, BF16),
        scratch_shapes=[pltpu.SemaphoreType.DMA((len(shifts),))],
        input_output_aliases={len(pieces) + 1: 0},
        compiler_params=PARAMS,
        name="place",
    )(here, *pieces, whole)


def ring(value, shift):
    size = lax.axis_size("z")
    return lax.ppermute(value, "z", [(i, (i + shift) % size) for i in range(size)])


def body(temps, sensors):
    tiers, snaps, width = temps.shape
    depth = tiers * snaps
    n_z, n_plane, devices = (lax.axis_size(a) for a in ("z", PLANE, AXES))
    per_z = sensors.shape[1] // n_z
    piece = per_z // n_plane
    z, xl = lax.axis_index("z"), lax.axis_index("xl")

    pixels = temps.reshape(depth, width)
    up, down = [pixels, ring(pixels, 1)], [pixels, ring(pixels, -1)]

    def go_on(ready):
        above, below, _ = lax.optimization_barrier((up[-1], down[-1], ready))
        up.append(ring(above, 1))
        down.append(ring(below, -1))

    first = lax.axis_index(AXES) * width
    column_first = first - z * lax.axis_size("xl") * width

    def part_of(number):
        start = number * SLOTS
        lists = compact(jnp.stack([first, start]), sensors, temps, n_z)
        lists = lax.all_to_all(lists, "z", 0, 0, tiled=True)
        return expand(jnp.stack([column_first, start, z * per_z]), sensors, lists, width)

    def summed_of(part):
        part = lax.all_to_all(part.reshape(n_plane, piece, depth), PLANE, 0, 0, tiled=True)
        part = part.astype(F32).sum(axis=0).astype(BF16)
        return jnp.broadcast_to(part[None], (n_plane, piece, depth))

    def handed_out(part):
        return lax.all_to_all(part, PLANE, 0, 0, tiled=True).reshape(per_z, depth)

    part = part_of(jnp.int32(0))
    go_on(part)
    seen, part = lax.optimization_barrier((sensors, part))
    part = summed_of(part)
    go_on(part)
    readings = handed_out(part)
    rounds = pl.cdiv(longest(seen, n_z, devices, width), SLOTS)
    _, readings = lax.while_loop(
        lambda state: state[0] < rounds,
        lambda state: (state[0] + 1, state[1] + handed_out(summed_of(part_of(state[0])))),
        (jnp.int32(1), readings),
    )

    here = jnp.stack([z, xl])

    def swapped(sent):
        return lax.ppermute(sent, "xl", [(0, 1), (1, 0)])

    near = [(block,) for block in (pixels, up[1], down[1], up[2], down[2])]
    late = [(up[3],), (down[3],)]
    shifts = [0, -1, 1, -2, 2, -3, 3, 4]
    sent = send(here, readings, near)
    above, below, _ = lax.optimization_barrier((up[3], down[3], sent))
    middle = depth // 2
    far = [(ring(above[:middle], 1), ring(below[middle:], -1))]
    pieces = [swapped(sent), swapped(send(here, readings, late)), swapped(send(here, readings, far))]
    return place(here, pieces, shifts, keep(here, readings, near + late + far, shifts))


def solution(mesh):
    torus = Mesh(mesh.devices.reshape(8, 2, 2, 8, 2), AXES)
    return jax.shard_map(
        body,
        mesh=torus,
        in_specs=(P(None, None, AXES), P()),
        out_specs=P(("z", "xl"), ("y", "xh", "core")),
        check_vma=False,
    )
```

```python
import functools
import math

import jax
import jax.numpy as jnp
from jax import lax
from jax.experimental import pallas as pl
from jax.experimental.pallas import tpu as pltpu
from jax.sharding import Mesh
from jax.sharding import PartitionSpec as P

AXES = ("y", "xh", "core", "z", "xl")
PLANE = ("y", "xh", "xl", "core")
SLOTS = 32
F32, BF16 = jnp.float32, jnp.bfloat16
PARAMS = pltpu.CompilerParams(vmem_limit_bytes=16 * 2**20)
NT = (((1,), (1,)), ((), ()))
VMEM = pl.BlockSpec(memory_space=pltpu.VMEM)
SMEM = pl.BlockSpec(memory_space=pltpu.SMEM)
HBM = pl.BlockSpec(memory_space=pl.ANY)


def matmul(a, b, dims=(((1,), (0,)), ((), ()))):
    return lax.dot_general(a, b, dims, preferred_element_type=F32)


def ones(mask):
    return mask.astype(F32).astype(BF16)


def triangles(tiers, columns):
    upper = lax.broadcasted_iota(jnp.int32, (columns, columns), 0) < lax.broadcasted_iota(
        jnp.int32, (columns, columns), 1
    )
    lower = lax.broadcasted_iota(jnp.int32, (tiers, tiers), 0) > lax.broadcasted_iota(
        jnp.int32, (tiers, tiers), 1
    )
    return ones(upper), ones(lower)


def ranks(mask, upper, lower):
    mask = ones(mask)
    return matmul(mask, upper) + matmul(lower, mask).sum(axis=1, keepdims=True)


def compact_kernel(scalar_ref, sensors_ref, temps_ref, out_ref):
    n_z, half, _ = out_ref.shape
    tiers, _, width = temps_ref.shape
    slots, per_z = 2 * half, sensors_ref.shape[1] // n_z
    first, start = scalar_ref[0], scalar_ref[1]
    upper, lower = triangles(tiers, per_z)
    slot_ids = lax.broadcasted_iota(jnp.int32, (slots, per_z), 0)
    tier_ids = lax.broadcasted_iota(jnp.int32, (tiers, per_z), 0)
    spots = []
    for z in range(n_z):
        offset = sensors_ref[:, z * per_z : (z + 1) * per_z] - first
        mine = (offset >= 0) & (offset < width)
        slot = ranks(mine, upper, lower).astype(jnp.int32) - start
        slot = jnp.where(mine, slot, -1)
        spot = (offset + tier_ids * width + 1).astype(F32)
        found = jnp.zeros((slots, per_z), F32)
        for tier in range(tiers):
            row = slice(tier, tier + 1)
            found = found + jnp.where(slot[row] == slot_ids, spot[row], 0.0)
        spots.append(found.sum(axis=1, keepdims=True))
    spots = jnp.concatenate(spots, axis=0).astype(jnp.int32) - 1
    lanes = lax.broadcasted_iota(jnp.int32, (n_z * slots, width), 1)
    total = jnp.zeros((n_z * slots, temps_ref.shape[1]), F32)
    for tier in range(tiers):
        total = total + matmul(ones(spots - tier * width == lanes), temps_ref[tier], NT)
    for z in range(n_z):
        low = z * slots
        out_ref[z] = jnp.concatenate(
            [total[low : low + half], total[low + half : low + slots]], axis=1
        ).astype(BF16)


def compact(scalars, sensors, temps, n_z):
    return pl.pallas_call(
        compact_kernel,
        in_specs=[SMEM, VMEM, VMEM],
        out_specs=VMEM,
        out_shape=jax.ShapeDtypeStruct((n_z, SLOTS // 2, 2 * temps.shape[1]), BF16),
        compiler_params=PARAMS,
        name="compact",
    )(scalars, sensors, temps)


def expand_kernel(width, scalar_ref, sensors_ref, lists_ref, out_ref):
    n_z, half, wide = lists_ref.shape
    snaps = wide // 2
    tiers = sensors_ref.shape[0]
    per_z = out_ref.shape[0]
    first, start, stride = scalar_ref[0], scalar_ref[1], 2 * width
    own = pl.multiple_of(scalar_ref[2], per_z)
    upper, lower = triangles(tiers, per_z)
    offset = sensors_ref[:, pl.ds(own, per_z)] - first
    spot = jnp.full((tiers, per_z), -1, jnp.int32)
    for z in range(n_z):
        there = (offset >= z * stride) & (offset < z * stride + width)
        slot = ranks(there, upper, lower).astype(jnp.int32) - start
        code = jnp.where(slot < half, slot + z * half, slot + (n_z - 1 + z) * half)
        spot = jnp.where(there & (slot >= 0) & (slot < 2 * half), code, spot)
    eye = lax.broadcasted_iota(jnp.int32, (tiers, tiers), 0) == lax.broadcasted_iota(
        jnp.int32, (tiers, tiers), 1
    )
    column = lax.dot_general(
        spot.astype(F32).astype(BF16), ones(eye), (((0,), (0,)), ((), ())), preferred_element_type=F32
    ).astype(jnp.int32)
    lists = lists_ref[...].reshape(n_z * half, wide)
    lists = jnp.concatenate([lists[:, :snaps], lists[:, snaps:]], axis=0)
    lanes = lax.broadcasted_iota(jnp.int32, (per_z, 2 * n_z * half), 1)
    for tier in range(0, tiers, 2):
        pair = [matmul(ones(lanes == column[:, t : t + 1]), lists) for t in (tier, tier + 1)]
        out_ref[:, tier * snaps : (tier + 2) * snaps] = jnp.concatenate(pair, axis=1).astype(BF16)


def expand(scalars, sensors, lists, width):
    n_z, _, wide = lists.shape
    tiers, count = sensors.shape
    return pl.pallas_call(
        functools.partial(expand_kernel, width),
        in_specs=[SMEM, VMEM, VMEM],
        out_specs=VMEM,
        out_shape=jax.ShapeDtypeStruct((count // n_z, tiers * wide // 2), BF16),
        compiler_params=PARAMS,
        name="expand",
    )(scalars, sensors, lists)


def longest_kernel(n_z, devices, width, sensors_ref, out_ref):
    tiers, count = sensors_ref.shape
    per_z, low = count // n_z, 16
    high_ids = lax.broadcasted_iota(jnp.int32, (devices // low, per_z), 0)
    low_ids = lax.broadcasted_iota(jnp.int32, (low, per_z), 0)
    most = jnp.zeros((devices // low, low), F32)
    for z in range(n_z):
        owner = sensors_ref[:, z * per_z : (z + 1) * per_z] // width
        total = jnp.zeros_like(most)
        for tier in range(tiers):
            row = owner[tier : tier + 1]
            total = total + matmul(ones(row // low == high_ids), ones(row % low == low_ids), NT)
        most = jnp.maximum(most, total)
    out_ref[0, 0] = jnp.max(most).astype(jnp.int32)


def longest(sensors, n_z, devices, width):
    return pl.pallas_call(
        functools.partial(longest_kernel, n_z, devices, width),
        in_specs=[VMEM],
        out_specs=SMEM,
        out_shape=jax.ShapeDtypeStruct((1, 1), jnp.int32),
        compiler_params=PARAMS,
        cost_estimate=pl.CostEstimate(
            flops=2 * sensors.size * devices, bytes_accessed=4 * sensors.size, transcendentals=0
        ),
        name="longest",
    )(sensors)[0, 0]


def correlation(scale, readings, block):
    depth = readings.shape[1] // len(block)
    parts = [
        matmul(readings[:, i * depth : (i + 1) * depth], part[...]) for i, part in enumerate(block)
    ]
    return (sum(parts[1:], parts[0]) * scale).astype(BF16)


def half_of(readings_ref, side):
    rows = readings_ref.shape[0] // 2
    return readings_ref[pl.ds(pl.multiple_of(side * rows, rows), rows)]


def grouped(refs, sizes):
    refs = iter(refs)
    return [[next(refs) for _ in range(size)] for size in sizes]


def send_kernel(scale, sizes, scalar_ref, readings_ref, *rest):
    readings = half_of(readings_ref, 1 - scalar_ref[1])
    for spot, block in enumerate(grouped(rest[:-1], sizes)):
        rest[-1][spot] = correlation(scale, readings, block)


def keep_kernel(scale, n_z, shifts, sizes, scalar_ref, readings_ref, *rest):
    *refs, out_ref, made, stored = rest
    readings = half_of(readings_ref, scalar_ref[1])
    stores = []
    for spot, block in enumerate(grouped(refs, sizes)):
        made[spot] = correlation(scale, readings, block)
        stores.append(
            pltpu.make_async_copy(
                made.at[spot], columns(out_ref, n_z, shifts[spot], scalar_ref, 0), stored.at[spot]
            )
        )
        stores[-1].start()
    for store in stores:
        store.wait()


def columns(out_ref, n_z, shift, scalar_ref, other):
    width = out_ref.shape[1] // (2 * n_z)
    side = 1 - scalar_ref[1] if other else scalar_ref[1]
    spot = (2 * lax.rem(scalar_ref[0] + shift + n_z, n_z) + side) * width
    return out_ref.at[:, pl.ds(pl.multiple_of(spot, width), width)]


def place_kernel(n_z, shifts, scalar_ref, *rest):
    *pieces, _, out_ref, done = rest
    stores = []
    for piece in pieces:
        for i in range(piece.shape[0]):
            spot = len(stores)
            stores.append(
                pltpu.make_async_copy(
                    piece.at[i], columns(out_ref, n_z, shifts[spot], scalar_ref, 1), done.at[spot]
                )
            )
            stores[-1].start()
    for store in stores:
        store.wait()


def cost(blocks, rows):
    pixels = sum(part.size for block in blocks for part in block)
    return pl.CostEstimate(flops=2 * rows * pixels, bytes_accessed=2 * pixels, transcendentals=0)


def send(here, readings, blocks):
    rows, depth = readings.shape[0] // 2, readings.shape[1]
    parts = [part for block in blocks for part in block]
    return pl.pallas_call(
        functools.partial(send_kernel, 1.0 / math.sqrt(depth), [len(block) for block in blocks]),
        in_specs=[SMEM, VMEM] + [VMEM] * len(parts),
        out_specs=VMEM,
        out_shape=jax.ShapeDtypeStruct((len(blocks), rows, parts[0].shape[1]), BF16),
        cost_estimate=cost(blocks, rows),
        compiler_params=PARAMS,
        name="send",
    )(here, readings, *parts)


def keep(here, readings, blocks, shifts):
    rows, depth = readings.shape[0] // 2, readings.shape[1]
    parts = [part for block in blocks for part in block]
    count, width = len(blocks), parts[0].shape[1]
    return pl.pallas_call(
        functools.partial(
            keep_kernel, 1.0 / math.sqrt(depth), count, shifts, [len(block) for block in blocks]
        ),
        in_specs=[SMEM, VMEM] + [VMEM] * len(parts),
        out_specs=HBM,
        out_shape=jax.ShapeDtypeStruct((rows, 2 * count * width), BF16),
        scratch_shapes=[pltpu.VMEM((count, rows, width), BF16), pltpu.SemaphoreType.DMA((count,))],
        cost_estimate=cost(blocks, rows),
        compiler_params=PARAMS,
        name="keep",
    )(here, readings, *parts)


def place(here, pieces, shifts, whole):
    return pl.pallas_call(
        functools.partial(place_kernel, len(shifts), shifts),
        in_specs=[SMEM] + [HBM] * (len(pieces) + 1),
        out_specs=HBM,
        out_shape=jax.ShapeDtypeStruct(whole.shape, BF16),
        scratch_shapes=[pltpu.SemaphoreType.DMA((len(shifts),))],
        input_output_aliases={len(pieces) + 1: 0},
        compiler_params=PARAMS,
        name="place",
    )(here, *pieces, whole)


def ring(value, shift):
    size = lax.axis_size("z")
    return lax.ppermute(value, "z", [(i, (i + shift) % size) for i in range(size)])


def body(temps, sensors):
    tiers, snaps, width = temps.shape
    depth = tiers * snaps
    n_z, n_plane, devices = (lax.axis_size(a) for a in ("z", PLANE, AXES))
    per_z = sensors.shape[1] // n_z
    piece = per_z // n_plane
    z, xl = lax.axis_index("z"), lax.axis_index("xl")

    pixels = temps.reshape(depth, width)
    up, down = [pixels, ring(pixels, 1)], [pixels]

    def go_on(blocks, shift, ready):
        block, _ = lax.optimization_barrier((blocks[-1], ready))
        blocks.append(ring(block, shift))

    first = lax.axis_index(AXES) * width
    column_first = first - z * lax.axis_size("xl") * width

    def listed(number):
        return compact(jnp.stack([first, number * SLOTS]), sensors, temps, n_z)

    def exchanged(lists):
        return lax.all_to_all(lists, "z", 0, 0, tiled=True)

    def part_of(number, lists):
        scalars = jnp.stack([column_first, number * SLOTS, z * per_z])
        return expand(scalars, sensors, lists, width)

    def summed_of(part):
        part = lax.all_to_all(part.reshape(n_plane, piece, depth), PLANE, 0, 0, tiled=True)
        part = part.astype(F32).sum(axis=0).astype(BF16)
        return jnp.broadcast_to(part[None], (n_plane, piece, depth))

    def handed_out(part):
        return lax.all_to_all(part, PLANE, 0, 0, tiled=True).reshape(per_z, depth)

    def one_round(number):
        return handed_out(summed_of(part_of(number, exchanged(listed(number)))))

    lists = listed(jnp.int32(0))
    go_on(down, -1, lists)
    lists = exchanged(lists)
    go_on(up, 1, lists)
    part = part_of(jnp.int32(0), lists)
    go_on(down, -1, part)
    go_on(up, 1, part)
    seen, part = lax.optimization_barrier((sensors, part))
    part = summed_of(part)
    go_on(down, -1, part)
    go_on(up, 1, part)
    readings = handed_out(part)
    rounds = pl.cdiv(longest(seen, n_z, devices, width), SLOTS)
    _, readings = lax.while_loop(
        lambda state: state[0] < rounds,
        lambda state: (state[0] + 1, state[1] + one_round(state[0])),
        (jnp.int32(1), readings),
    )

    here = jnp.stack([z, xl])

    def swapped(sent):
        return lax.ppermute(sent, "xl", [(0, 1), (1, 0)])

    blocks = [(block,) for block in (*up[:2], down[1], up[2], down[2], up[3], down[3], up[4])]
    shifts = [0, -1, 1, -2, 2, -3, 3, 4]
    pieces = [swapped(send(here, readings, blocks[low:high])) for low, high in ((0, 6), (6, 8))]
    return place(here, pieces, shifts, keep(here, readings, blocks, shifts))


def solution(mesh):
    torus = Mesh(mesh.devices.reshape(8, 2, 2, 8, 2), AXES)
    return jax.shard_map(
        body,
        mesh=torus,
        in_specs=(P(None, None, AXES), P()),
        out_specs=P(("z", "xl"), ("y", "xh", "core")),
        check_vma=False,
    )
```

```python
import functools
import math

import jax
import jax.numpy as jnp
from jax import lax
from jax.experimental import pallas as pl
from jax.experimental.pallas import tpu as pltpu
from jax.sharding import Mesh
from jax.sharding import PartitionSpec as P

AXES = ("y", "xh", "core", "z", "xl")
LISTS = ("z", "xh", "xl", "core")
PLANE = ("xh", "xl", "core", "y")
SLOTS = 8
F32, BF16 = jnp.float32, jnp.bfloat16
PARAMS = pltpu.CompilerParams(vmem_limit_bytes=16 * 2**20)
NT = (((1,), (1,)), ((), ()))
VMEM = pl.BlockSpec(memory_space=pltpu.VMEM)
SMEM = pl.BlockSpec(memory_space=pltpu.SMEM)
HBM = pl.BlockSpec(memory_space=pl.ANY)


def matmul(a, b, dims=(((1,), (0,)), ((), ()))):
    return lax.dot_general(a, b, dims, preferred_element_type=F32)


def ones(mask):
    return mask.astype(F32).astype(BF16)


def compact_kernel(scalar_ref, sensors_ref, temps_ref, out_ref):
    tiers, snaps, width = temps_ref.shape
    count, rows = sensors_ref.shape[1], out_ref.shape[0]
    span = 256
    group = count * SLOTS // rows
    first, start = scalar_ref[0], scalar_ref[1]
    before = lax.broadcasted_iota(jnp.int32, (span, span), 0)
    after = lax.broadcasted_iota(jnp.int32, (span, span), 1)
    together = before // group == after // group
    ahead, together = ones(together & (before < after)), ones(together)
    lower = ones(
        lax.broadcasted_iota(jnp.int32, (tiers, tiers), 0)
        > lax.broadcasted_iota(jnp.int32, (tiers, tiers), 1)
    )
    made = span * SLOTS // group
    row_ids = lax.broadcasted_iota(jnp.int32, (made, span), 0)
    tier_ids = lax.broadcasted_iota(jnp.int32, (tiers, span), 0)
    list_ids = lax.broadcasted_iota(jnp.int32, (tiers, span), 1) // group
    spots = []
    for low in range(0, count, span):
        offset = sensors_ref[:, low : low + span] - first
        mine = (offset >= 0) & (offset < width)
        held = ones(mine)
        slot = matmul(held, ahead) + matmul(matmul(lower, held).astype(BF16), together)
        slot = slot.astype(jnp.int32) - start
        slot = jnp.where(mine & (slot >= 0) & (slot < SLOTS), slot + list_ids * SLOTS, -1)
        spot = (offset + tier_ids * width + 1).astype(F32)
        found = jnp.zeros((made, span), F32)
        for tier in range(tiers):
            row = slice(tier, tier + 1)
            found = found + jnp.where(slot[row] == row_ids, spot[row], 0.0)
        spots.append(found.sum(axis=1, keepdims=True))
    spots = jnp.concatenate(spots, axis=0).astype(jnp.int32) - 1
    lanes = lax.broadcasted_iota(jnp.int32, (rows, width), 1)
    total = jnp.zeros((rows, snaps), F32)
    for tier in range(tiers):
        total = total + matmul(ones(spots - tier * width == lanes), temps_ref[tier], NT)
    out_ref[...] = jnp.concatenate([total, jnp.zeros_like(total)], axis=1).astype(BF16)


def compact(scalars, sensors, temps, lists):
    snaps = temps.shape[1]
    return pl.pallas_call(
        compact_kernel,
        in_specs=[SMEM, VMEM, VMEM],
        out_specs=VMEM,
        out_shape=jax.ShapeDtypeStruct((lists * SLOTS, 2 * snaps), BF16),
        compiler_params=PARAMS,
        name="compact",
    )(scalars, sensors, temps).reshape(lists, SLOTS, 2 * snaps)


def expand_kernel(shift, scalar_ref, rows_ref, columns_ref, lists_ref, out_ref):
    tiers, group = rows_ref.shape
    n_lists, slots, wide = lists_ref.shape
    y, start = scalar_ref[0], scalar_ref[1]
    rows, owners = rows_ref[...] >> shift, columns_ref[...] >> shift
    later = lax.broadcasted_iota(jnp.int32, (group, group), 0) > lax.broadcasted_iota(
        jnp.int32, (group, group), 1
    )
    lists = lists_ref[...].reshape(n_lists * slots, wide)
    lanes = lax.broadcasted_iota(jnp.int32, (group, n_lists * slots), 1)
    found = []
    for tier in range(tiers):
        owner = owners[:, tier : tier + 1]
        same = [(owner == rows[t : t + 1]).astype(F32) for t in range(tier + 1)]
        same[-1] = jnp.where(later, same[-1], 0.0)
        slot = sum(same[1:], same[0]).sum(axis=1, keepdims=True).astype(jnp.int32) - start
        sender = (owner >> 1 & 7) * 8 + (owner >> 5 & 1) * 4 + (owner & 1) * 2 + (owner >> 4 & 1)
        there = (owner >> 6 == y) & (slot >= 0) & (slot < slots)
        spot = jnp.where(there, sender * slots + slot, -1)
        found.append(matmul(ones(spot == lanes), lists)[:, : wide // 2])
    for tier in range(0, tiers, 2):
        pair = jnp.concatenate(found[tier : tier + 2], axis=1)
        out_ref[:, tier * wide // 2 : (tier + 2) * wide // 2] = pair.astype(BF16)


def expand(scalars, chosen, lists, width):
    tiers, group = chosen.shape
    return pl.pallas_call(
        functools.partial(expand_kernel, width.bit_length() - 1),
        in_specs=[SMEM, VMEM, VMEM, VMEM],
        out_specs=VMEM,
        out_shape=jax.ShapeDtypeStruct((group, tiers * lists.shape[2] // 2), BF16),
        compiler_params=PARAMS,
        name="expand",
    )(scalars, chosen, chosen.T, lists)


def longest_kernel(group, devices, shift, sensors_ref, out_ref):
    tiers, count = sensors_ref.shape
    span, low = 256, 16
    lists = span // group
    high_ids = lax.broadcasted_iota(jnp.int32, (devices // low, span), 0)
    low_ids = lax.broadcasted_iota(jnp.int32, (low * lists, span), 0)
    list_ids = lax.broadcasted_iota(jnp.int32, (1, span), 1) // group
    most = jnp.zeros((devices // low, low * lists), F32)
    for at in range(0, count, span):
        owner = sensors_ref[:, at : at + span] >> shift
        total = jnp.zeros_like(most)
        for tier in range(tiers):
            row = owner[tier : tier + 1]
            lows = (row & low - 1) + list_ids * low
            total = total + matmul(ones(row >> 4 == high_ids), ones(lows == low_ids), NT)
        most = jnp.maximum(most, total)
    out_ref[0, 0] = jnp.max(most).astype(jnp.int32)


def longest(sensors, group, devices, width):
    return pl.pallas_call(
        functools.partial(longest_kernel, group, devices, width.bit_length() - 1),
        in_specs=[VMEM],
        out_specs=SMEM,
        out_shape=jax.ShapeDtypeStruct((1, 1), jnp.int32),
        cost_estimate=pl.CostEstimate(
            flops=2 * sensors.size * devices, bytes_accessed=4 * sensors.size, transcendentals=0
        ),
        compiler_params=PARAMS,
        name="longest",
    )(sensors)[0, 0]


def correlation(scale, readings, block):
    depth = readings.shape[1] // len(block)
    parts = [
        matmul(readings[:, i * depth : (i + 1) * depth], part[...]) for i, part in enumerate(block)
    ]
    return (sum(parts[1:], parts[0]) * scale).astype(BF16)


def half_of(readings_ref, side):
    rows = readings_ref.shape[0] // 2
    return readings_ref[pl.ds(pl.multiple_of(side * rows, rows), rows)]


def grouped(refs, sizes):
    refs = iter(refs)
    return [[next(refs) for _ in range(size)] for size in sizes]


def send_kernel(scale, sizes, scalar_ref, readings_ref, *rest):
    readings = half_of(readings_ref, 1 - scalar_ref[1])
    for spot, block in enumerate(grouped(rest[:-1], sizes)):
        rest[-1][spot] = correlation(scale, readings, block)


def keep_kernel(scale, n_z, shifts, sizes, scalar_ref, readings_ref, *rest):
    *refs, out_ref, made, stored = rest
    readings = half_of(readings_ref, scalar_ref[1])
    stores = []
    for spot, block in enumerate(grouped(refs, sizes)):
        made[spot] = correlation(scale, readings, block)
        stores.append(
            pltpu.make_async_copy(
                made.at[spot], columns(out_ref, n_z, shifts[spot], scalar_ref, 0), stored.at[spot]
            )
        )
        stores[-1].start()
    for store in stores:
        store.wait()


def columns(out_ref, n_z, shift, scalar_ref, other):
    width = out_ref.shape[1] // (2 * n_z)
    side = 1 - scalar_ref[1] if other else scalar_ref[1]
    spot = (2 * lax.rem(scalar_ref[0] + shift + n_z, n_z) + side) * width
    return out_ref.at[:, pl.ds(pl.multiple_of(spot, width), width)]


def place_kernel(n_z, shifts, scalar_ref, *rest):
    *pieces, _, out_ref, done = rest
    stores = []
    for piece in pieces:
        for i in range(piece.shape[0]):
            spot = len(stores)
            stores.append(
                pltpu.make_async_copy(
                    piece.at[i], columns(out_ref, n_z, shifts[spot], scalar_ref, 1), done.at[spot]
                )
            )
            stores[-1].start()
    for store in stores:
        store.wait()


def cost(blocks, rows):
    pixels = sum(part.size for block in blocks for part in block)
    return pl.CostEstimate(flops=2 * rows * pixels, bytes_accessed=2 * pixels, transcendentals=0)


def send(here, readings, blocks):
    rows, depth = readings.shape[0] // 2, readings.shape[1]
    parts = [part for block in blocks for part in block]
    return pl.pallas_call(
        functools.partial(send_kernel, 1.0 / math.sqrt(depth), [len(block) for block in blocks]),
        in_specs=[SMEM, VMEM] + [VMEM] * len(parts),
        out_specs=VMEM,
        out_shape=jax.ShapeDtypeStruct((len(blocks), rows, parts[0].shape[1]), BF16),
        cost_estimate=cost(blocks, rows),
        compiler_params=PARAMS,
        name="send",
    )(here, readings, *parts)


def keep(here, readings, blocks, shifts):
    rows, depth = readings.shape[0] // 2, readings.shape[1]
    parts = [part for block in blocks for part in block]
    count, width = len(blocks), parts[0].shape[1]
    return pl.pallas_call(
        functools.partial(
            keep_kernel, 1.0 / math.sqrt(depth), count, shifts, [len(block) for block in blocks]
        ),
        in_specs=[SMEM, VMEM] + [VMEM] * len(parts),
        out_specs=HBM,
        out_shape=jax.ShapeDtypeStruct((rows, 2 * count * width), BF16),
        scratch_shapes=[pltpu.VMEM((count, rows, width), BF16), pltpu.SemaphoreType.DMA((count,))],
        cost_estimate=cost(blocks, rows),
        compiler_params=PARAMS,
        name="keep",
    )(here, readings, *parts)


def place(here, pieces, shifts, whole):
    return pl.pallas_call(
        functools.partial(place_kernel, len(shifts), shifts),
        in_specs=[SMEM] + [HBM] * (len(pieces) + 1),
        out_specs=HBM,
        out_shape=jax.ShapeDtypeStruct(whole.shape, BF16),
        scratch_shapes=[pltpu.SemaphoreType.DMA((len(shifts),))],
        input_output_aliases={len(pieces) + 1: 0},
        compiler_params=PARAMS,
        name="place",
    )(here, *pieces, whole)


def ring(value, shift):
    size = lax.axis_size("z")
    return lax.ppermute(value, "z", [(i, (i + shift) % size) for i in range(size)])


def body(temps, sensors):
    tiers, snaps, width = temps.shape
    depth = tiers * snaps
    n_z, n_y, n_lists, n_plane, devices = (lax.axis_size(a) for a in ("z", "y", LISTS, PLANE, AXES))
    group = sensors.shape[1] // n_lists
    z, xl = lax.axis_index("z"), lax.axis_index("xl")

    pixels = temps.reshape(depth, width)
    up, down = [pixels, ring(pixels, 1)], [pixels, ring(pixels, -1)]

    def go_on(blocks, shift, ready):
        block, _ = lax.optimization_barrier((blocks[-1], ready))
        blocks.append(ring(block, shift))

    first = lax.axis_index(AXES) * width
    def listed(number):
        return compact(jnp.stack([first, number * SLOTS]), sensors, temps, n_lists)

    def exchanged(lists):
        return lax.all_to_all(lists, LISTS, 0, 0, tiled=True)

    chosen = lax.dynamic_slice_in_dim(sensors, lax.axis_index(LISTS) * group, group, axis=1)

    def part_of(number, lists):
        return expand(jnp.stack([lax.axis_index("y"), number * SLOTS]), chosen, lists, width)

    def summed_of(part):
        part = lax.all_to_all(part.reshape(n_y, group // n_y, depth), "y", 0, 0, tiled=True)
        part = part.astype(F32).sum(axis=0).astype(BF16)
        return jnp.broadcast_to(part[None], (n_plane, *part.shape))

    def handed_out(part):
        return lax.all_to_all(part, PLANE, 0, 0, tiled=True).reshape(-1, depth)

    def one_round(number):
        return handed_out(summed_of(part_of(number, exchanged(listed(number)))))

    part = part_of(jnp.int32(0), exchanged(listed(jnp.int32(0))))
    go_on(up, 1, part)
    go_on(down, -1, part)
    part = summed_of(part)
    seen, _ = lax.optimization_barrier((sensors, part))
    rounds = pl.cdiv(longest(seen, group, devices, width), SLOTS)
    go_on(up, 1, part)
    go_on(down, -1, part)
    readings = handed_out(part)
    _, readings = lax.while_loop(
        lambda state: state[0] < rounds,
        lambda state: (state[0] + 1, state[1] + one_round(state[0])),
        (jnp.int32(1), readings),
    )

    here = jnp.stack([z, xl])

    def swapped(sent):
        return lax.ppermute(sent, "xl", [(0, 1), (1, 0)])

    sent = send(here, readings, [(block,) for block in (pixels, up[1], down[1], up[2], down[2])])
    above, below, _ = lax.optimization_barrier((up[3], down[3], sent))
    middle = depth // 2
    far = (ring(above[:middle], 1), ring(below[middle:], -1))
    blocks = [(block,) for block in (*up[:2], down[1], up[2], down[2], up[3], down[3])] + [far]
    shifts = [0, -1, 1, -2, 2, -3, 3, 4]
    pieces = [swapped(sent)]
    pieces += [swapped(send(here, readings, blocks[low:high])) for low, high in ((5, 7), (7, 8))]
    return place(here, pieces, shifts, keep(here, readings, blocks, shifts))


def solution(mesh):
    torus = Mesh(mesh.devices.reshape(8, 2, 2, 8, 2), AXES)
    return jax.shard_map(
        body,
        mesh=torus,
        in_specs=(P(None, None, AXES), P()),
        out_specs=P(("z", "xl"), ("y", "xh", "core")),
        check_vma=False,
    )
```

```python
import functools
import math

import jax
import jax.numpy as jnp
from jax import lax
from jax.experimental import pallas as pl
from jax.experimental.pallas import tpu as pltpu
from jax.sharding import Mesh
from jax.sharding import PartitionSpec as P

AXES = ("y", "xh", "core", "z", "xl")
LISTS = ("z", "xh", "xl", "core")
PLANE = ("xh", "xl", "core", "y")
SLOTS = 8
F32, BF16 = jnp.float32, jnp.bfloat16
PARAMS = pltpu.CompilerParams(vmem_limit_bytes=16 * 2**20)
NT = (((1,), (1,)), ((), ()))
VMEM = pl.BlockSpec(memory_space=pltpu.VMEM)
SMEM = pl.BlockSpec(memory_space=pltpu.SMEM)
HBM = pl.BlockSpec(memory_space=pl.ANY)


def matmul(a, b, dims=(((1,), (0,)), ((), ()))):
    return lax.dot_general(a, b, dims, preferred_element_type=F32)


def ones(mask):
    return mask.astype(F32).astype(BF16)


def compact_kernel(scalar_ref, sensors_ref, temps_ref, out_ref):
    tiers, snaps, width = temps_ref.shape
    count, rows = sensors_ref.shape[1], out_ref.shape[0]
    span = 256
    group = count * SLOTS // rows
    first, start = scalar_ref[0], scalar_ref[1]
    before = lax.broadcasted_iota(jnp.int32, (span, span), 0)
    after = lax.broadcasted_iota(jnp.int32, (span, span), 1)
    together = before // group == after // group
    ahead, together = ones(together & (before < after)), ones(together)
    lower = ones(
        lax.broadcasted_iota(jnp.int32, (tiers, tiers), 0)
        > lax.broadcasted_iota(jnp.int32, (tiers, tiers), 1)
    )
    made = span * SLOTS // group
    row_ids = lax.broadcasted_iota(jnp.int32, (made, span), 0)
    tier_ids = lax.broadcasted_iota(jnp.int32, (tiers, span), 0)
    list_ids = lax.broadcasted_iota(jnp.int32, (tiers, span), 1) // group
    spots = []
    for low in range(0, count, span):
        offset = sensors_ref[:, low : low + span] - first
        mine = (offset >= 0) & (offset < width)
        held = ones(mine)
        slot = matmul(held, ahead) + matmul(matmul(lower, held).astype(BF16), together)
        slot = slot.astype(jnp.int32) - start
        slot = jnp.where(mine & (slot >= 0) & (slot < SLOTS), slot + list_ids * SLOTS, -1)
        spot = (offset + tier_ids * width + 1).astype(F32)
        found = jnp.zeros((made, span), F32)
        for tier in range(tiers):
            row = slice(tier, tier + 1)
            found = found + jnp.where(slot[row] == row_ids, spot[row], 0.0)
        spots.append(found.sum(axis=1, keepdims=True))
    spots = jnp.concatenate(spots, axis=0).astype(jnp.int32) - 1
    lanes = lax.broadcasted_iota(jnp.int32, (rows, width), 1)
    total = jnp.zeros((rows, snaps), F32)
    for tier in range(tiers):
        total = total + matmul(ones(spots - tier * width == lanes), temps_ref[tier], NT)
    out_ref[...] = jnp.concatenate([total, jnp.zeros_like(total)], axis=1).astype(BF16)


def compact(scalars, sensors, temps, lists):
    snaps = temps.shape[1]
    return pl.pallas_call(
        compact_kernel,
        in_specs=[SMEM, VMEM, VMEM],
        out_specs=VMEM,
        out_shape=jax.ShapeDtypeStruct((lists * SLOTS, 2 * snaps), BF16),
        compiler_params=PARAMS,
        name="compact",
    )(scalars, sensors, temps).reshape(lists, SLOTS, 2 * snaps)


def expand_kernel(shift, scalar_ref, rows_ref, columns_ref, lists_ref, out_ref):
    tiers, group = rows_ref.shape
    n_lists, slots, wide = lists_ref.shape
    y, start = scalar_ref[0], scalar_ref[1]
    rows, owners = rows_ref[...] >> shift, columns_ref[...] >> shift
    later = lax.broadcasted_iota(jnp.int32, (group, group), 0) > lax.broadcasted_iota(
        jnp.int32, (group, group), 1
    )
    lists = lists_ref[...].reshape(n_lists * slots, wide)
    lanes = lax.broadcasted_iota(jnp.int32, (group, n_lists * slots), 1)
    found = []
    for tier in range(tiers):
        owner = owners[:, tier : tier + 1]
        same = [(owner == rows[t : t + 1]).astype(F32) for t in range(tier + 1)]
        same[-1] = jnp.where(later, same[-1], 0.0)
        slot = sum(same[1:], same[0]).sum(axis=1, keepdims=True).astype(jnp.int32) - start
        sender = (owner >> 1 & 7) * 8 + (owner >> 5 & 1) * 4 + (owner & 1) * 2 + (owner >> 4 & 1)
        there = (owner >> 6 == y) & (slot >= 0) & (slot < slots)
        spot = jnp.where(there, sender * slots + slot, -1)
        found.append(matmul(ones(spot == lanes), lists)[:, : wide // 2])
    for tier in range(0, tiers, 2):
        pair = jnp.concatenate(found[tier : tier + 2], axis=1)
        out_ref[:, tier * wide // 2 : (tier + 2) * wide // 2] = pair.astype(BF16)


def expand(scalars, chosen, turned, lists, width):
    tiers, group = chosen.shape
    return pl.pallas_call(
        functools.partial(expand_kernel, width.bit_length() - 1),
        in_specs=[SMEM, VMEM, VMEM, VMEM],
        out_specs=VMEM,
        out_shape=jax.ShapeDtypeStruct((group, tiers * lists.shape[2] // 2), BF16),
        compiler_params=PARAMS,
        name="expand",
    )(scalars, chosen, turned, lists)


def longest_kernel(group, devices, shift, sensors_ref, out_ref):
    tiers, count = sensors_ref.shape
    span, low = 256, 16
    lists = span // group
    high_ids = lax.broadcasted_iota(jnp.int32, (devices // low, span), 0)
    low_ids = lax.broadcasted_iota(jnp.int32, (low * lists, span), 0)
    list_ids = lax.broadcasted_iota(jnp.int32, (1, span), 1) // group
    most = jnp.zeros((devices // low, low * lists), F32)
    for at in range(0, count, span):
        owner = sensors_ref[:, at : at + span] >> shift
        total = jnp.zeros_like(most)
        for tier in range(tiers):
            row = owner[tier : tier + 1]
            lows = (row & low - 1) + list_ids * low
            total = total + matmul(ones(row >> 4 == high_ids), ones(lows == low_ids), NT)
        most = jnp.maximum(most, total)
    out_ref[0, 0] = jnp.max(most).astype(jnp.int32)


def longest(sensors, group, devices, width):
    return pl.pallas_call(
        functools.partial(longest_kernel, group, devices, width.bit_length() - 1),
        in_specs=[VMEM],
        out_specs=SMEM,
        out_shape=jax.ShapeDtypeStruct((1, 1), jnp.int32),
        cost_estimate=pl.CostEstimate(
            flops=100 * sensors.size * devices, bytes_accessed=4 * sensors.size, transcendentals=0
        ),
        compiler_params=PARAMS,
        name="longest",
    )(sensors)[0, 0]


def correlation(scale, readings, block):
    depth = readings.shape[1] // len(block)
    parts = [
        matmul(readings[:, i * depth : (i + 1) * depth], part[...]) for i, part in enumerate(block)
    ]
    return (sum(parts[1:], parts[0]) * scale).astype(BF16)


def half_of(readings_ref, side):
    rows = readings_ref.shape[0] // 2
    return readings_ref[pl.ds(pl.multiple_of(side * rows, rows), rows)]


def grouped(refs, sizes):
    refs = iter(refs)
    return [[next(refs) for _ in range(size)] for size in sizes]


def send_kernel(scale, sizes, scalar_ref, readings_ref, *rest):
    readings = half_of(readings_ref, 1 - scalar_ref[1])
    for spot, block in enumerate(grouped(rest[:-1], sizes)):
        rest[-1][spot] = correlation(scale, readings, block)


def keep_kernel(scale, n_z, shifts, sizes, scalar_ref, readings_ref, *rest):
    *refs, out_ref, made, stored = rest
    readings = half_of(readings_ref, scalar_ref[1])
    stores = []
    for spot, block in enumerate(grouped(refs, sizes)):
        made[spot] = correlation(scale, readings, block)
        stores.append(
            pltpu.make_async_copy(
                made.at[spot], columns(out_ref, n_z, shifts[spot], scalar_ref, 0), stored.at[spot]
            )
        )
        stores[-1].start()
    for store in stores:
        store.wait()


def columns(out_ref, n_z, shift, scalar_ref, other):
    width = out_ref.shape[1] // (2 * n_z)
    side = 1 - scalar_ref[1] if other else scalar_ref[1]
    spot = (2 * lax.rem(scalar_ref[0] + shift + n_z, n_z) + side) * width
    return out_ref.at[:, pl.ds(pl.multiple_of(spot, width), width)]


def place_kernel(n_z, shifts, scalar_ref, *rest):
    *pieces, _, out_ref, done = rest
    stores = []
    for piece in pieces:
        for i in range(piece.shape[0]):
            spot = len(stores)
            stores.append(
                pltpu.make_async_copy(
                    piece.at[i], columns(out_ref, n_z, shifts[spot], scalar_ref, 1), done.at[spot]
                )
            )
            stores[-1].start()
    for store in stores:
        store.wait()


def cost(blocks, rows):
    pixels = sum(part.size for block in blocks for part in block)
    return pl.CostEstimate(flops=2 * rows * pixels, bytes_accessed=2 * pixels, transcendentals=0)


def send(here, readings, blocks):
    rows, depth = readings.shape[0] // 2, readings.shape[1]
    parts = [part for block in blocks for part in block]
    return pl.pallas_call(
        functools.partial(send_kernel, 1.0 / math.sqrt(depth), [len(block) for block in blocks]),
        in_specs=[SMEM, VMEM] + [VMEM] * len(parts),
        out_specs=VMEM,
        out_shape=jax.ShapeDtypeStruct((len(blocks), rows, parts[0].shape[1]), BF16),
        cost_estimate=cost(blocks, rows),
        compiler_params=PARAMS,
        name="send",
    )(here, readings, *parts)


def keep(here, readings, blocks, shifts):
    rows, depth = readings.shape[0] // 2, readings.shape[1]
    parts = [part for block in blocks for part in block]
    count, width = len(blocks), parts[0].shape[1]
    return pl.pallas_call(
        functools.partial(
            keep_kernel, 1.0 / math.sqrt(depth), count, shifts, [len(block) for block in blocks]
        ),
        in_specs=[SMEM, VMEM] + [VMEM] * len(parts),
        out_specs=HBM,
        out_shape=jax.ShapeDtypeStruct((rows, 2 * count * width), BF16),
        scratch_shapes=[pltpu.VMEM((count, rows, width), BF16), pltpu.SemaphoreType.DMA((count,))],
        cost_estimate=cost(blocks, rows),
        compiler_params=PARAMS,
        name="keep",
    )(here, readings, *parts)


def place(here, pieces, shifts, whole):
    return pl.pallas_call(
        functools.partial(place_kernel, len(shifts), shifts),
        in_specs=[SMEM] + [HBM] * (len(pieces) + 1),
        out_specs=HBM,
        out_shape=jax.ShapeDtypeStruct(whole.shape, BF16),
        scratch_shapes=[pltpu.SemaphoreType.DMA((len(shifts),))],
        input_output_aliases={len(pieces) + 1: 0},
        compiler_params=PARAMS,
        name="place",
    )(here, *pieces, whole)


def ring(value, shift):
    size = lax.axis_size("z")
    return lax.ppermute(value, "z", [(i, (i + shift) % size) for i in range(size)])


def body(temps, sensors):
    tiers, snaps, width = temps.shape
    depth = tiers * snaps
    n_z, n_y, n_lists, n_plane, devices = (lax.axis_size(a) for a in ("z", "y", LISTS, PLANE, AXES))
    group = sensors.shape[1] // n_lists
    z, xl = lax.axis_index("z"), lax.axis_index("xl")

    pixels = temps.reshape(depth, width)
    near = [ring(pixels, shift) for shift in (1, -1)]

    def after(ready, *values):
        return lax.optimization_barrier((*values, ready))[:-1]

    first = lax.axis_index(AXES) * width
    chosen = lax.dynamic_slice_in_dim(sensors, lax.axis_index(LISTS) * group, group, axis=1)
    chosen, turned, sensors = lax.optimization_barrier((chosen, chosen.T, sensors))

    def listed(number):
        return compact(jnp.stack([first, number * SLOTS]), sensors, temps, n_lists)

    def exchanged(lists):
        return lax.all_to_all(lists, LISTS, 0, 0, tiled=True)

    def part_of(number, lists):
        return expand(jnp.stack([lax.axis_index("y"), number * SLOTS]), chosen, turned, lists, width)

    def summed_of(part):
        part = lax.all_to_all(part.reshape(n_y, group // n_y, depth), "y", 0, 0, tiled=True)
        part = part.astype(F32).sum(axis=0).astype(BF16)
        return jnp.broadcast_to(part[None], (n_plane, *part.shape))

    def handed_out(part):
        return lax.all_to_all(part, PLANE, 0, 0, tiled=True).reshape(-1, depth)

    def one_round(number):
        return handed_out(summed_of(part_of(number, exchanged(listed(number)))))

    lists = listed(jnp.int32(0))
    (again,) = after(lists, pixels)
    second = [ring(again, shift) for shift in (2, -2)]
    part = summed_of(part_of(jnp.int32(0), exchanged(lists)))
    above, below, seen = after(part, *second, sensors)
    third = [ring(above, 1), ring(below, -1)]
    middle = depth // 2
    far = (ring(above[:middle], 2), ring(below[middle:], -2))
    readings = handed_out(part)
    rounds = pl.cdiv(longest(seen, group, devices, width), SLOTS)
    _, readings = lax.while_loop(
        lambda state: state[0] < rounds,
        lambda state: (state[0] + 1, state[1] + one_round(state[0])),
        (jnp.int32(1), readings),
    )

    here = jnp.stack([z, xl])

    def swapped(sent):
        return lax.ppermute(sent, "xl", [(0, 1), (1, 0)])

    blocks = [(block,) for block in (pixels, *near, *second, *third)] + [far]
    shifts = [0, -1, 1, -2, 2, -3, 3, 4]
    pieces = [
        swapped(send(here, readings, blocks[low:high])) for low, high in ((0, 5), (5, 7), (7, 8))
    ]
    return place(here, pieces, shifts, keep(here, readings, blocks, shifts))


def solution(mesh):
    torus = Mesh(mesh.devices.reshape(8, 2, 2, 8, 2), AXES)
    return jax.shard_map(
        body,
        mesh=torus,
        in_specs=(P(None, None, AXES), P()),
        out_specs=P(("z", "xl"), ("y", "xh", "core")),
        check_vma=False,
    )
```

```python
import functools
import math

import jax
import jax.numpy as jnp
from jax import lax
from jax.experimental import pallas as pl
from jax.experimental.pallas import tpu as pltpu
from jax.sharding import Mesh
from jax.sharding import PartitionSpec as P

AXES = ("y", "xh", "core", "z", "xl")
LISTS = ("z", "xh", "xl", "core")
PLANE = ("xh", "xl", "core", "y")
SLOTS = 8
F32, BF16 = jnp.float32, jnp.bfloat16
PARAMS = pltpu.CompilerParams(vmem_limit_bytes=16 * 2**20)
NT = (((1,), (1,)), ((), ()))
VMEM = pl.BlockSpec(memory_space=pltpu.VMEM)
SMEM = pl.BlockSpec(memory_space=pltpu.SMEM)
HBM = pl.BlockSpec(memory_space=pl.ANY)


def matmul(a, b, dims=(((1,), (0,)), ((), ()))):
    return lax.dot_general(a, b, dims, preferred_element_type=F32)


def ones(mask):
    return mask.astype(F32).astype(BF16)


def compact_kernel(scalar_ref, sensors_ref, temps_ref, out_ref):
    tiers, snaps, width = temps_ref.shape
    count, rows = sensors_ref.shape[1], out_ref.shape[0]
    span = 256
    group = count * SLOTS // rows
    first, start = scalar_ref[0], scalar_ref[1]
    before = lax.broadcasted_iota(jnp.int32, (span, span), 0)
    after = lax.broadcasted_iota(jnp.int32, (span, span), 1)
    together = before // group == after // group
    ahead, together = ones(together & (before < after)), ones(together)
    lower = ones(
        lax.broadcasted_iota(jnp.int32, (tiers, tiers), 0)
        > lax.broadcasted_iota(jnp.int32, (tiers, tiers), 1)
    )
    made = span * SLOTS // group
    row_ids = lax.broadcasted_iota(jnp.int32, (made, span), 0)
    tier_ids = lax.broadcasted_iota(jnp.int32, (tiers, span), 0)
    list_ids = lax.broadcasted_iota(jnp.int32, (tiers, span), 1) // group
    spots = []
    for low in range(0, count, span):
        offset = sensors_ref[:, low : low + span] - first
        mine = (offset >= 0) & (offset < width)
        held = ones(mine)
        slot = matmul(held, ahead) + matmul(matmul(lower, held).astype(BF16), together)
        slot = slot.astype(jnp.int32) - start
        slot = jnp.where(mine & (slot >= 0) & (slot < SLOTS), slot + list_ids * SLOTS, -1)
        spot = (offset + tier_ids * width + 1).astype(F32)
        found = jnp.zeros((made, span), F32)
        for tier in range(tiers):
            row = slice(tier, tier + 1)
            found = found + jnp.where(slot[row] == row_ids, spot[row], 0.0)
        spots.append(found.sum(axis=1, keepdims=True))
    spots = jnp.concatenate(spots, axis=0).astype(jnp.int32) - 1
    lanes = lax.broadcasted_iota(jnp.int32, (rows, width), 1)
    total = jnp.zeros((rows, snaps), F32)
    for tier in range(tiers):
        total = total + matmul(ones(spots - tier * width == lanes), temps_ref[tier], NT)
    out_ref[...] = jnp.concatenate([total, jnp.zeros_like(total)], axis=1).astype(BF16)


def compact(scalars, sensors, temps, lists):
    snaps = temps.shape[1]
    return pl.pallas_call(
        compact_kernel,
        in_specs=[SMEM, VMEM, VMEM],
        out_specs=VMEM,
        out_shape=jax.ShapeDtypeStruct((lists * SLOTS, 2 * snaps), BF16),
        compiler_params=PARAMS,
        name="compact",
    )(scalars, sensors, temps).reshape(lists, SLOTS, 2 * snaps)


def expand_kernel(shift, scalar_ref, rows_ref, columns_ref, lists_ref, out_ref):
    tiers, group = rows_ref.shape
    n_lists, slots, wide = lists_ref.shape
    y, start = scalar_ref[0], scalar_ref[1]
    rows, owners = rows_ref[...] >> shift, columns_ref[...] >> shift
    later = lax.broadcasted_iota(jnp.int32, (group, group), 0) > lax.broadcasted_iota(
        jnp.int32, (group, group), 1
    )
    lists = lists_ref[...].reshape(n_lists * slots, wide)
    lanes = lax.broadcasted_iota(jnp.int32, (group, n_lists * slots), 1)
    found = []
    for tier in range(tiers):
        owner = owners[:, tier : tier + 1]
        same = [(owner == rows[t : t + 1]).astype(F32) for t in range(tier + 1)]
        same[-1] = jnp.where(later, same[-1], 0.0)
        slot = sum(same[1:], same[0]).sum(axis=1, keepdims=True).astype(jnp.int32) - start
        sender = (owner >> 1 & 7) * 8 + (owner >> 5 & 1) * 4 + (owner & 1) * 2 + (owner >> 4 & 1)
        there = (owner >> 6 == y) & (slot >= 0) & (slot < slots)
        spot = jnp.where(there, sender * slots + slot, -1)
        found.append(matmul(ones(spot == lanes), lists)[:, : wide // 2])
    for tier in range(0, tiers, 2):
        pair = jnp.concatenate(found[tier : tier + 2], axis=1)
        out_ref[:, tier * wide // 2 : (tier + 2) * wide // 2] = pair.astype(BF16)


def expand(scalars, chosen, lists, width):
    tiers, group = chosen.shape
    return pl.pallas_call(
        functools.partial(expand_kernel, width.bit_length() - 1),
        in_specs=[SMEM, VMEM, VMEM, VMEM],
        out_specs=VMEM,
        out_shape=jax.ShapeDtypeStruct((group, tiers * lists.shape[2] // 2), BF16),
        compiler_params=PARAMS,
        name="expand",
    )(scalars, chosen, chosen.T, lists)


def longest_kernel(group, devices, shift, sensors_ref, out_ref):
    tiers, count = sensors_ref.shape
    span, low = 256, 16
    lists = span // group
    high_ids = lax.broadcasted_iota(jnp.int32, (devices // low, span), 0)
    low_ids = lax.broadcasted_iota(jnp.int32, (low * lists, span), 0)
    list_ids = lax.broadcasted_iota(jnp.int32, (1, span), 1) // group
    most = jnp.zeros((devices // low, low * lists), F32)
    for at in range(0, count, span):
        owner = sensors_ref[:, at : at + span] >> shift
        total = jnp.zeros_like(most)
        for tier in range(tiers):
            row = owner[tier : tier + 1]
            lows = (row & low - 1) + list_ids * low
            total = total + matmul(ones(row >> 4 == high_ids), ones(lows == low_ids), NT)
        most = jnp.maximum(most, total)
    out_ref[0, 0] = jnp.max(most).astype(jnp.int32)


def longest(sensors, group, devices, width):
    return pl.pallas_call(
        functools.partial(longest_kernel, group, devices, width.bit_length() - 1),
        in_specs=[VMEM],
        out_specs=SMEM,
        out_shape=jax.ShapeDtypeStruct((1, 1), jnp.int32),
        cost_estimate=pl.CostEstimate(
            flops=100 * sensors.size * devices, bytes_accessed=4 * sensors.size, transcendentals=0
        ),
        compiler_params=PARAMS,
        name="longest",
    )(sensors)[0, 0]


def correlation(scale, readings, block):
    depth = readings.shape[1] // len(block)
    parts = [
        matmul(readings[:, i * depth : (i + 1) * depth], part[...]) for i, part in enumerate(block)
    ]
    return (sum(parts[1:], parts[0]) * scale).astype(BF16)


def half_of(readings_ref, side):
    rows = readings_ref.shape[0] // 2
    return readings_ref[pl.ds(pl.multiple_of(side * rows, rows), rows)]


def grouped(refs, sizes):
    refs = iter(refs)
    return [[next(refs) for _ in range(size)] for size in sizes]


def send_kernel(scale, sizes, scalar_ref, readings_ref, *rest):
    readings = half_of(readings_ref, 1 - scalar_ref[1])
    for spot, block in enumerate(grouped(rest[:-1], sizes)):
        rest[-1][spot] = correlation(scale, readings, block)


def keep_kernel(scale, n_z, shifts, sizes, scalar_ref, readings_ref, *rest):
    *refs, out_ref, made, stored = rest
    readings = half_of(readings_ref, scalar_ref[1])
    stores = []
    for spot, block in enumerate(grouped(refs, sizes)):
        made[spot] = correlation(scale, readings, block)
        stores.append(
            pltpu.make_async_copy(
                made.at[spot], columns(out_ref, n_z, shifts[spot], scalar_ref, 0), stored.at[spot]
            )
        )
        stores[-1].start()
    for store in stores:
        store.wait()


def columns(out_ref, n_z, shift, scalar_ref, other):
    width = out_ref.shape[1] // (2 * n_z)
    side = 1 - scalar_ref[1] if other else scalar_ref[1]
    spot = (2 * lax.rem(scalar_ref[0] + shift + n_z, n_z) + side) * width
    return out_ref.at[:, pl.ds(pl.multiple_of(spot, width), width)]


def place_kernel(n_z, shifts, scalar_ref, *rest):
    *pieces, _, out_ref, done = rest
    stores = []
    for piece in pieces:
        for i in range(piece.shape[0]):
            spot = len(stores)
            stores.append(
                pltpu.make_async_copy(
                    piece.at[i], columns(out_ref, n_z, shifts[spot], scalar_ref, 1), done.at[spot]
                )
            )
            stores[-1].start()
    for store in stores:
        store.wait()


def cost(blocks, rows):
    pixels = sum(part.size for block in blocks for part in block)
    return pl.CostEstimate(flops=2 * rows * pixels, bytes_accessed=2 * pixels, transcendentals=0)


def send(here, readings, blocks):
    rows, depth = readings.shape[0] // 2, readings.shape[1]
    parts = [part for block in blocks for part in block]
    return pl.pallas_call(
        functools.partial(send_kernel, 1.0 / math.sqrt(depth), [len(block) for block in blocks]),
        in_specs=[SMEM, VMEM] + [VMEM] * len(parts),
        out_specs=VMEM,
        out_shape=jax.ShapeDtypeStruct((len(blocks), rows, parts[0].shape[1]), BF16),
        cost_estimate=cost(blocks, rows),
        compiler_params=PARAMS,
        name="send",
    )(here, readings, *parts)


def keep(here, readings, blocks, shifts):
    rows, depth = readings.shape[0] // 2, readings.shape[1]
    parts = [part for block in blocks for part in block]
    count, width = len(blocks), parts[0].shape[1]
    return pl.pallas_call(
        functools.partial(
            keep_kernel, 1.0 / math.sqrt(depth), count, shifts, [len(block) for block in blocks]
        ),
        in_specs=[SMEM, VMEM] + [VMEM] * len(parts),
        out_specs=HBM,
        out_shape=jax.ShapeDtypeStruct((rows, 2 * count * width), BF16),
        scratch_shapes=[pltpu.VMEM((count, rows, width), BF16), pltpu.SemaphoreType.DMA((count,))],
        cost_estimate=cost(blocks, rows),
        compiler_params=PARAMS,
        name="keep",
    )(here, readings, *parts)


def place(here, pieces, shifts, whole):
    return pl.pallas_call(
        functools.partial(place_kernel, len(shifts), shifts),
        in_specs=[SMEM] + [HBM] * (len(pieces) + 1),
        out_specs=HBM,
        out_shape=jax.ShapeDtypeStruct(whole.shape, BF16),
        scratch_shapes=[pltpu.SemaphoreType.DMA((len(shifts),))],
        input_output_aliases={len(pieces) + 1: 0},
        compiler_params=PARAMS,
        name="place",
    )(here, *pieces, whole)


def ring(value, shift):
    size = lax.axis_size("z")
    return lax.ppermute(value, "z", [(i, (i + shift) % size) for i in range(size)])


def body(temps, sensors):
    tiers, snaps, width = temps.shape
    depth = tiers * snaps
    n_z, n_y, n_lists, n_plane, devices = (lax.axis_size(a) for a in ("z", "y", LISTS, PLANE, AXES))
    group = sensors.shape[1] // n_lists
    z, xl = lax.axis_index("z"), lax.axis_index("xl")

    pixels = temps.reshape(depth, width)
    up, down = [pixels, ring(pixels, 1)], [pixels, ring(pixels, -1)]

    def go_on(blocks, shift, ready):
        block, _ = lax.optimization_barrier((blocks[-1], ready))
        blocks.append(ring(block, shift))

    first = lax.axis_index(AXES) * width
    def listed(number):
        return compact(jnp.stack([first, number * SLOTS]), sensors, temps, n_lists)

    def exchanged(lists):
        return lax.all_to_all(lists, LISTS, 0, 0, tiled=True)

    chosen = lax.dynamic_slice_in_dim(sensors, lax.axis_index(LISTS) * group, group, axis=1)

    def part_of(number, lists):
        return expand(jnp.stack([lax.axis_index("y"), number * SLOTS]), chosen, lists, width)

    lists = listed(jnp.int32(0))
    seen, _ = lax.optimization_barrier((sensors, lists))
    rounds = pl.cdiv(longest(seen, group, devices, width), SLOTS)
    _, part = lax.while_loop(
        lambda state: state[0] < rounds,
        lambda state: (state[0] + 1, state[1] + part_of(state[0], exchanged(listed(state[0])))),
        (jnp.int32(1), part_of(jnp.int32(0), exchanged(lists))),
    )
    go_on(up, 1, part)
    go_on(down, -1, part)
    part = lax.all_to_all(part.reshape(n_y, group // n_y, depth), "y", 0, 0, tiled=True)
    part = part.astype(F32).sum(axis=0).astype(BF16)
    go_on(up, 1, part)
    go_on(down, -1, part)
    copies = jnp.broadcast_to(part[None], (n_plane, *part.shape))
    readings = lax.all_to_all(copies, PLANE, 0, 0, tiled=True).reshape(-1, depth)

    here = jnp.stack([z, xl])

    def swapped(sent):
        return lax.ppermute(sent, "xl", [(0, 1), (1, 0)])

    sent = send(here, readings, [(block,) for block in (pixels, up[1], down[1], up[2], down[2])])
    above, below, _ = lax.optimization_barrier((up[3], down[3], sent))
    middle = depth // 2
    far = (ring(above[:middle], 1), ring(below[middle:], -1))
    blocks = [(block,) for block in (*up[:2], down[1], up[2], down[2], up[3], down[3])] + [far]
    shifts = [0, -1, 1, -2, 2, -3, 3, 4]
    pieces = [swapped(sent)]
    pieces += [swapped(send(here, readings, blocks[low:high])) for low, high in ((5, 7), (7, 8))]
    return place(here, pieces, shifts, keep(here, readings, blocks, shifts))


def solution(mesh):
    torus = Mesh(mesh.devices.reshape(8, 2, 2, 8, 2), AXES)
    return jax.shard_map(
        body,
        mesh=torus,
        in_specs=(P(None, None, AXES), P()),
        out_specs=P(("z", "xl"), ("y", "xh", "core")),
        check_vma=False,
    )
```

```python
import functools
import math

import jax
import jax.numpy as jnp
from jax import lax
from jax.experimental import pallas as pl
from jax.experimental.pallas import tpu as pltpu
from jax.sharding import Mesh
from jax.sharding import PartitionSpec as P

AXES = ("y", "xh", "core", "z", "xl")
LISTS = ("z", "y")
SIDE = ("xh", "xl", "core")
PLANE = ("y", "xh", "xl", "core")
SLOTS = 8
F32, BF16 = jnp.float32, jnp.bfloat16
PARAMS = pltpu.CompilerParams(vmem_limit_bytes=16 * 2**20)
NT = (((1,), (1,)), ((), ()))
VMEM = pl.BlockSpec(memory_space=pltpu.VMEM)
SMEM = pl.BlockSpec(memory_space=pltpu.SMEM)
HBM = pl.BlockSpec(memory_space=pl.ANY)


def matmul(a, b, dims=(((1,), (0,)), ((), ()))):
    return lax.dot_general(a, b, dims, preferred_element_type=F32)


def ones(mask):
    return mask.astype(F32).astype(BF16)


def compact_kernel(scalar_ref, sensors_ref, temps_ref, out_ref):
    tiers, snaps, width = temps_ref.shape
    count, rows = sensors_ref.shape[1], out_ref.shape[0]
    span = 256
    group = count * SLOTS // rows
    first, start = scalar_ref[0], scalar_ref[1]
    before = lax.broadcasted_iota(jnp.int32, (span, span), 0)
    after = lax.broadcasted_iota(jnp.int32, (span, span), 1)
    together = before // group == after // group
    ahead, together = ones(together & (before < after)), ones(together)
    lower = ones(
        lax.broadcasted_iota(jnp.int32, (tiers, tiers), 0)
        > lax.broadcasted_iota(jnp.int32, (tiers, tiers), 1)
    )
    made = span * SLOTS // group
    row_ids = lax.broadcasted_iota(jnp.int32, (made, span), 0)
    tier_ids = lax.broadcasted_iota(jnp.int32, (tiers, span), 0)
    list_ids = lax.broadcasted_iota(jnp.int32, (tiers, span), 1) // group
    spots = []
    for low in range(0, count, span):
        offset = sensors_ref[:, low : low + span] - first
        mine = (offset >= 0) & (offset < width)
        held = ones(mine)
        slot = matmul(held, ahead) + matmul(matmul(lower, held).astype(BF16), together)
        slot = slot.astype(jnp.int32) - start
        slot = jnp.where(mine & (slot >= 0) & (slot < SLOTS), slot + list_ids * SLOTS, -1)
        spot = (offset + tier_ids * width + 1).astype(F32)
        found = jnp.zeros((made, span), F32)
        for tier in range(tiers):
            row = slice(tier, tier + 1)
            found = found + jnp.where(slot[row] == row_ids, spot[row], 0.0)
        spots.append(found.sum(axis=1, keepdims=True))
    spots = jnp.concatenate(spots, axis=0).astype(jnp.int32) - 1
    lanes = lax.broadcasted_iota(jnp.int32, (rows, width), 1)
    total = jnp.zeros((rows, snaps), F32)
    for tier in range(tiers):
        total = total + matmul(ones(spots - tier * width == lanes), temps_ref[tier], NT)
    out_ref[...] = jnp.concatenate([total, jnp.zeros_like(total)], axis=1).astype(BF16)


def compact(scalars, sensors, temps, lists):
    snaps = temps.shape[1]
    return pl.pallas_call(
        compact_kernel,
        in_specs=[SMEM, VMEM, VMEM],
        out_specs=VMEM,
        out_shape=jax.ShapeDtypeStruct((lists * SLOTS, 2 * snaps), BF16),
        compiler_params=PARAMS,
        name="compact",
    )(scalars, sensors, temps).reshape(lists, SLOTS, 2 * snaps)


def expand_kernel(shift, scalar_ref, rows_ref, columns_ref, lists_ref, out_ref):
    tiers, group = rows_ref.shape
    n_lists, slots, wide = lists_ref.shape
    side, start = scalar_ref[0], scalar_ref[1]
    rows, owners = rows_ref[...] >> shift, columns_ref[...] >> shift
    later = lax.broadcasted_iota(jnp.int32, (group, group), 0) > lax.broadcasted_iota(
        jnp.int32, (group, group), 1
    )
    lists = lists_ref[...].reshape(n_lists * slots, wide)
    lanes = lax.broadcasted_iota(jnp.int32, (group, n_lists * slots), 1)
    found = []
    for tier in range(tiers):
        owner = owners[:, tier : tier + 1]
        same = [(owner == rows[t : t + 1]).astype(F32) for t in range(tier + 1)]
        same[-1] = jnp.where(later, same[-1], 0.0)
        slot = sum(same[1:], same[0]).sum(axis=1, keepdims=True).astype(jnp.int32) - start
        sender = (owner >> 1 & 7) * 8 + (owner >> 6)
        there = (owner & 49 == side) & (slot >= 0) & (slot < slots)
        spot = jnp.where(there, sender * slots + slot, -1)
        found.append(matmul(ones(spot == lanes), lists)[:, : wide // 2])
    for tier in range(0, tiers, 2):
        pair = jnp.concatenate(found[tier : tier + 2], axis=1)
        out_ref[:, tier * wide // 2 : (tier + 2) * wide // 2] = pair.astype(BF16)


def expand(scalars, chosen, lists, width):
    tiers, group = chosen.shape
    return pl.pallas_call(
        functools.partial(expand_kernel, width.bit_length() - 1),
        in_specs=[SMEM, VMEM, VMEM, VMEM],
        out_specs=VMEM,
        out_shape=jax.ShapeDtypeStruct((group, tiers * lists.shape[2] // 2), BF16),
        compiler_params=PARAMS,
        name="expand",
    )(scalars, chosen, chosen.T, lists)


def longest_kernel(group, devices, shift, sensors_ref, out_ref):
    tiers, count = sensors_ref.shape
    span, low = 256, 16
    lists = span // group
    high_ids = lax.broadcasted_iota(jnp.int32, (devices // low, span), 0)
    low_ids = lax.broadcasted_iota(jnp.int32, (low * lists, span), 0)
    list_ids = lax.broadcasted_iota(jnp.int32, (1, span), 1) // group
    most = jnp.zeros((devices // low, low * lists), F32)
    for at in range(0, count, span):
        owner = sensors_ref[:, at : at + span] >> shift
        total = jnp.zeros_like(most)
        for tier in range(tiers):
            row = owner[tier : tier + 1]
            lows = (row & low - 1) + list_ids * low
            total = total + matmul(ones(row >> 4 == high_ids), ones(lows == low_ids), NT)
        most = jnp.maximum(most, total)
    out_ref[0, 0] = jnp.max(most).astype(jnp.int32)


def longest(sensors, group, devices, width):
    return pl.pallas_call(
        functools.partial(longest_kernel, group, devices, width.bit_length() - 1),
        in_specs=[VMEM],
        out_specs=SMEM,
        out_shape=jax.ShapeDtypeStruct((1, 1), jnp.int32),
        cost_estimate=pl.CostEstimate(
            flops=100 * sensors.size * devices, bytes_accessed=4 * sensors.size, transcendentals=0
        ),
        compiler_params=PARAMS,
        name="longest",
    )(sensors)[0, 0]


def correlation(scale, readings, block):
    depth = readings.shape[1] // len(block)
    parts = [
        matmul(readings[:, i * depth : (i + 1) * depth], part[...]) for i, part in enumerate(block)
    ]
    return (sum(parts[1:], parts[0]) * scale).astype(BF16)


def half_of(readings_ref, side):
    rows = readings_ref.shape[0] // 2
    return readings_ref[pl.ds(pl.multiple_of(side * rows, rows), rows)]


def grouped(refs, sizes):
    refs = iter(refs)
    return [[next(refs) for _ in range(size)] for size in sizes]


def send_kernel(scale, sizes, scalar_ref, readings_ref, *rest):
    readings = half_of(readings_ref, 1 - scalar_ref[1])
    for spot, block in enumerate(grouped(rest[:-1], sizes)):
        rest[-1][spot] = correlation(scale, readings, block)


def keep_kernel(scale, n_z, shifts, sizes, scalar_ref, readings_ref, *rest):
    *refs, out_ref, made, stored = rest
    readings = half_of(readings_ref, scalar_ref[1])
    stores = []
    for spot, block in enumerate(grouped(refs, sizes)):
        made[spot] = correlation(scale, readings, block)
        stores.append(
            pltpu.make_async_copy(
                made.at[spot], columns(out_ref, n_z, shifts[spot], scalar_ref, 0), stored.at[spot]
            )
        )
        stores[-1].start()
    for store in stores:
        store.wait()


def columns(out_ref, n_z, shift, scalar_ref, other):
    width = out_ref.shape[1] // (2 * n_z)
    side = 1 - scalar_ref[1] if other else scalar_ref[1]
    spot = (2 * lax.rem(scalar_ref[0] + shift + n_z, n_z) + side) * width
    return out_ref.at[:, pl.ds(pl.multiple_of(spot, width), width)]


def place_kernel(n_z, shifts, scalar_ref, *rest):
    *pieces, _, out_ref, done = rest
    stores = []
    for piece in pieces:
        for i in range(piece.shape[0]):
            spot = len(stores)
            stores.append(
                pltpu.make_async_copy(
                    piece.at[i], columns(out_ref, n_z, shifts[spot], scalar_ref, 1), done.at[spot]
                )
            )
            stores[-1].start()
    for store in stores:
        store.wait()


def cost(blocks, rows):
    pixels = sum(part.size for block in blocks for part in block)
    return pl.CostEstimate(flops=2 * rows * pixels, bytes_accessed=2 * pixels, transcendentals=0)


def send(here, readings, blocks):
    rows, depth = readings.shape[0] // 2, readings.shape[1]
    parts = [part for block in blocks for part in block]
    return pl.pallas_call(
        functools.partial(send_kernel, 1.0 / math.sqrt(depth), [len(block) for block in blocks]),
        in_specs=[SMEM, VMEM] + [VMEM] * len(parts),
        out_specs=VMEM,
        out_shape=jax.ShapeDtypeStruct((len(blocks), rows, parts[0].shape[1]), BF16),
        cost_estimate=cost(blocks, rows),
        compiler_params=PARAMS,
        name="send",
    )(here, readings, *parts)


def keep(here, readings, blocks, shifts):
    rows, depth = readings.shape[0] // 2, readings.shape[1]
    parts = [part for block in blocks for part in block]
    count, width = len(blocks), parts[0].shape[1]
    return pl.pallas_call(
        functools.partial(
            keep_kernel, 1.0 / math.sqrt(depth), count, shifts, [len(block) for block in blocks]
        ),
        in_specs=[SMEM, VMEM] + [VMEM] * len(parts),
        out_specs=HBM,
        out_shape=jax.ShapeDtypeStruct((rows, 2 * count * width), BF16),
        scratch_shapes=[pltpu.VMEM((count, rows, width), BF16), pltpu.SemaphoreType.DMA((count,))],
        cost_estimate=cost(blocks, rows),
        compiler_params=PARAMS,
        name="keep",
    )(here, readings, *parts)


def place(here, pieces, shifts, whole):
    return pl.pallas_call(
        functools.partial(place_kernel, len(shifts), shifts),
        in_specs=[SMEM] + [HBM] * (len(pieces) + 1),
        out_specs=HBM,
        out_shape=jax.ShapeDtypeStruct(whole.shape, BF16),
        scratch_shapes=[pltpu.SemaphoreType.DMA((len(shifts),))],
        input_output_aliases={len(pieces) + 1: 0},
        compiler_params=PARAMS,
        name="place",
    )(here, *pieces, whole)


def ring(value, shift):
    size = lax.axis_size("z")
    return lax.ppermute(value, "z", [(i, (i + shift) % size) for i in range(size)])


def body(temps, sensors):
    tiers, snaps, width = temps.shape
    depth = tiers * snaps
    n_side, n_lists, n_plane, devices = (lax.axis_size(a) for a in (SIDE, LISTS, PLANE, AXES))
    group = sensors.shape[1] // n_lists
    z, xl = lax.axis_index("z"), lax.axis_index("xl")

    pixels = temps.reshape(depth, width)
    up, down = [pixels, ring(pixels, 1)], [pixels, ring(pixels, -1)]

    def go_on(blocks, shift, ready):
        block, _ = lax.optimization_barrier((blocks[-1], ready))
        blocks.append(ring(block, shift))

    first = lax.axis_index(AXES) * width
    side = lax.axis_index("xh") * 32 + lax.axis_index("core") * 16 + xl
    def listed(number):
        return compact(jnp.stack([first, number * SLOTS]), sensors, temps, n_lists)

    def exchanged(lists):
        return lax.all_to_all(lists, LISTS, 0, 0, tiled=True)

    chosen = lax.dynamic_slice_in_dim(sensors, lax.axis_index(LISTS) * group, group, axis=1)

    def part_of(number, lists):
        return expand(jnp.stack([side, number * SLOTS]), chosen, lists, width)

    lists = listed(jnp.int32(0))
    seen, _ = lax.optimization_barrier((sensors, lists))
    rounds = pl.cdiv(longest(seen, group, devices, width), SLOTS)
    _, part = lax.while_loop(
        lambda state: state[0] < rounds,
        lambda state: (state[0] + 1, state[1] + part_of(state[0], exchanged(listed(state[0])))),
        (jnp.int32(1), part_of(jnp.int32(0), exchanged(lists))),
    )
    go_on(up, 1, part)
    go_on(down, -1, part)
    part = lax.all_to_all(part.reshape(n_side, group // n_side, depth), SIDE, 0, 0, tiled=True)
    part = part.astype(F32).sum(axis=0).astype(BF16)
    go_on(up, 1, part)
    go_on(down, -1, part)
    copies = jnp.broadcast_to(part[None], (n_plane, *part.shape))
    readings = lax.all_to_all(copies, PLANE, 0, 0, tiled=True).reshape(-1, depth)

    here = jnp.stack([z, xl])

    def swapped(sent):
        return lax.ppermute(sent, "xl", [(0, 1), (1, 0)])

    sent = send(here, readings, [(block,) for block in (pixels, up[1], down[1], up[2], down[2])])
    above, below, _ = lax.optimization_barrier((up[3], down[3], sent))
    middle = depth // 2
    far = (ring(above[:middle], 1), ring(below[middle:], -1))
    blocks = [(block,) for block in (*up[:2], down[1], up[2], down[2], up[3], down[3])] + [far]
    shifts = [0, -1, 1, -2, 2, -3, 3, 4]
    pieces = [swapped(sent)]
    pieces += [swapped(send(here, readings, blocks[low:high])) for low, high in ((5, 7), (7, 8))]
    return place(here, pieces, shifts, keep(here, readings, blocks, shifts))


def solution(mesh):
    torus = Mesh(mesh.devices.reshape(8, 2, 2, 8, 2), AXES)
    return jax.shard_map(
        body,
        mesh=torus,
        in_specs=(P(None, None, AXES), P()),
        out_specs=P(("z", "xl"), ("y", "xh", "core")),
        check_vma=False,
    )
```

```python
import functools
import math

import jax
import jax.numpy as jnp
from jax import lax
from jax.experimental import pallas as pl
from jax.experimental.pallas import tpu as pltpu
from jax.sharding import Mesh
from jax.sharding import PartitionSpec as P

AXES = ("y", "xh", "core", "z", "xl")
LISTS = ("z", "y")
SIDE = ("xh", "xl", "core")
PLANE = ("y", "xh", "xl", "core")
SLOTS = 8
F32, BF16 = jnp.float32, jnp.bfloat16
PARAMS = pltpu.CompilerParams(vmem_limit_bytes=16 * 2**20)
NT = (((1,), (1,)), ((), ()))
VMEM = pl.BlockSpec(memory_space=pltpu.VMEM)
SMEM = pl.BlockSpec(memory_space=pltpu.SMEM)
HBM = pl.BlockSpec(memory_space=pl.ANY)


def matmul(a, b, dims=(((1,), (0,)), ((), ()))):
    return lax.dot_general(a, b, dims, preferred_element_type=F32)


def ones(mask):
    return mask.astype(F32).astype(BF16)


def compact_kernel(scalar_ref, sensors_ref, temps_ref, out_ref):
    tiers, snaps, width = temps_ref.shape
    count, rows = sensors_ref.shape[1], out_ref.shape[0]
    span = 256
    group = count * SLOTS // rows
    first, start = scalar_ref[0], scalar_ref[1]
    before = lax.broadcasted_iota(jnp.int32, (span, span), 0)
    after = lax.broadcasted_iota(jnp.int32, (span, span), 1)
    together = before // group == after // group
    ahead, together = ones(together & (before < after)), ones(together)
    lower = ones(
        lax.broadcasted_iota(jnp.int32, (tiers, tiers), 0)
        > lax.broadcasted_iota(jnp.int32, (tiers, tiers), 1)
    )
    made = span * SLOTS // group
    row_ids = lax.broadcasted_iota(jnp.int32, (made, span), 0)
    tier_ids = lax.broadcasted_iota(jnp.int32, (tiers, span), 0)
    list_ids = lax.broadcasted_iota(jnp.int32, (tiers, span), 1) // group
    spots = []
    for low in range(0, count, span):
        offset = sensors_ref[:, low : low + span] - first
        mine = (offset >= 0) & (offset < width)
        held = ones(mine)
        slot = matmul(held, ahead) + matmul(matmul(lower, held).astype(BF16), together)
        slot = slot.astype(jnp.int32) - start
        slot = jnp.where(mine & (slot >= 0) & (slot < SLOTS), slot + list_ids * SLOTS, -1)
        spot = (offset + tier_ids * width + 1).astype(F32)
        found = jnp.zeros((made, span), F32)
        for tier in range(tiers):
            row = slice(tier, tier + 1)
            found = found + jnp.where(slot[row] == row_ids, spot[row], 0.0)
        spots.append(found.sum(axis=1, keepdims=True))
    spots = jnp.concatenate(spots, axis=0).astype(jnp.int32) - 1
    lanes = lax.broadcasted_iota(jnp.int32, (rows, width), 1)
    total = jnp.zeros((rows, snaps), F32)
    for tier in range(tiers):
        total = total + matmul(ones(spots - tier * width == lanes), temps_ref[tier], NT)
    out_ref[...] = jnp.concatenate([total, jnp.zeros_like(total)], axis=1).astype(BF16)


def compact(scalars, sensors, temps, lists):
    snaps = temps.shape[1]
    return pl.pallas_call(
        compact_kernel,
        in_specs=[SMEM, VMEM, VMEM],
        out_specs=VMEM,
        out_shape=jax.ShapeDtypeStruct((lists * SLOTS, 2 * snaps), BF16),
        compiler_params=PARAMS,
        name="compact",
    )(scalars, sensors, temps).reshape(lists, SLOTS, 2 * snaps)


def expand_kernel(shift, scalar_ref, rows_ref, columns_ref, lists_ref, out_ref):
    tiers, group = rows_ref.shape
    n_lists, slots, wide = lists_ref.shape
    side, start = scalar_ref[0], scalar_ref[1]
    rows, owners = rows_ref[...] >> shift, columns_ref[...] >> shift
    later = lax.broadcasted_iota(jnp.int32, (group, group), 0) > lax.broadcasted_iota(
        jnp.int32, (group, group), 1
    )
    lists = lists_ref[...].reshape(n_lists * slots, wide)
    lanes = lax.broadcasted_iota(jnp.int32, (group, n_lists * slots), 1)
    found = []
    for tier in range(tiers):
        owner = owners[:, tier : tier + 1]
        same = [(owner == rows[t : t + 1]).astype(F32) for t in range(tier + 1)]
        same[-1] = jnp.where(later, same[-1], 0.0)
        slot = sum(same[1:], same[0]).sum(axis=1, keepdims=True).astype(jnp.int32) - start
        sender = (owner >> 1 & 7) * 8 + (owner >> 6)
        there = (owner & 49 == side) & (slot >= 0) & (slot < slots)
        spot = jnp.where(there, sender * slots + slot, -1)
        found.append(matmul(ones(spot == lanes), lists)[:, : wide // 2])
    for tier in range(0, tiers, 2):
        pair = jnp.concatenate(found[tier : tier + 2], axis=1)
        out_ref[:, tier * wide // 2 : (tier + 2) * wide // 2] = pair.astype(BF16)


def expand(scalars, chosen, lists, width):
    tiers, group = chosen.shape
    return pl.pallas_call(
        functools.partial(expand_kernel, width.bit_length() - 1),
        in_specs=[SMEM, VMEM, VMEM, VMEM],
        out_specs=VMEM,
        out_shape=jax.ShapeDtypeStruct((group, tiers * lists.shape[2] // 2), BF16),
        compiler_params=PARAMS,
        name="expand",
    )(scalars, chosen, chosen.T, lists)


def longest_kernel(group, devices, shift, sensors_ref, out_ref):
    tiers, count = sensors_ref.shape
    span, low = 256, 16
    lists = span // group
    high_ids = lax.broadcasted_iota(jnp.int32, (devices // low, span), 0)
    low_ids = lax.broadcasted_iota(jnp.int32, (low * lists, span), 0)
    list_ids = lax.broadcasted_iota(jnp.int32, (1, span), 1) // group
    most = jnp.zeros((devices // low, low * lists), F32)
    for at in range(0, count, span):
        owner = sensors_ref[:, at : at + span] >> shift
        total = jnp.zeros_like(most)
        for tier in range(tiers):
            row = owner[tier : tier + 1]
            lows = (row & low - 1) + list_ids * low
            total = total + matmul(ones(row >> 4 == high_ids), ones(lows == low_ids), NT)
        most = jnp.maximum(most, total)
    out_ref[0, 0] = jnp.max(most).astype(jnp.int32)


def longest(sensors, group, devices, width):
    return pl.pallas_call(
        functools.partial(longest_kernel, group, devices, width.bit_length() - 1),
        in_specs=[VMEM],
        out_specs=SMEM,
        out_shape=jax.ShapeDtypeStruct((1, 1), jnp.int32),
        cost_estimate=pl.CostEstimate(
            flops=100 * sensors.size * devices, bytes_accessed=4 * sensors.size, transcendentals=0
        ),
        compiler_params=PARAMS,
        name="longest",
    )(sensors)[0, 0]


def correlation(scale, readings, block):
    depth = readings.shape[1] // len(block)
    parts = [
        matmul(readings[:, i * depth : (i + 1) * depth], part[...]) for i, part in enumerate(block)
    ]
    return (sum(parts[1:], parts[0]) * scale).astype(BF16)


def half_of(readings_ref, side):
    rows = readings_ref.shape[0] // 2
    return readings_ref[pl.ds(pl.multiple_of(side * rows, rows), rows)]


def grouped(refs, sizes):
    refs = iter(refs)
    return [[next(refs) for _ in range(size)] for size in sizes]


def send_kernel(scale, sizes, scalar_ref, readings_ref, *rest):
    readings = half_of(readings_ref, 1 - scalar_ref[1])
    for spot, block in enumerate(grouped(rest[:-1], sizes)):
        rest[-1][spot] = correlation(scale, readings, block)


def keep_kernel(scale, n_z, shifts, sizes, scalar_ref, readings_ref, *rest):
    *refs, out_ref, made, stored = rest
    readings = half_of(readings_ref, scalar_ref[1])
    stores = []
    for spot, block in enumerate(grouped(refs, sizes)):
        made[spot] = correlation(scale, readings, block)
        stores.append(
            pltpu.make_async_copy(
                made.at[spot], columns(out_ref, n_z, shifts[spot], scalar_ref, 0), stored.at[spot]
            )
        )
        stores[-1].start()
    for store in stores:
        store.wait()


def columns(out_ref, n_z, shift, scalar_ref, other):
    width = out_ref.shape[1] // (2 * n_z)
    side = 1 - scalar_ref[1] if other else scalar_ref[1]
    spot = (2 * lax.rem(scalar_ref[0] + shift + n_z, n_z) + side) * width
    return out_ref.at[:, pl.ds(pl.multiple_of(spot, width), width)]


def place_kernel(n_z, shifts, scalar_ref, *rest):
    *pieces, _, out_ref, done = rest
    stores = []
    for piece in pieces:
        for i in range(piece.shape[0]):
            spot = len(stores)
            stores.append(
                pltpu.make_async_copy(
                    piece.at[i], columns(out_ref, n_z, shifts[spot], scalar_ref, 1), done.at[spot]
                )
            )
            stores[-1].start()
    for store in stores:
        store.wait()


def cost(blocks, rows):
    pixels = sum(part.size for block in blocks for part in block)
    return pl.CostEstimate(flops=2 * rows * pixels, bytes_accessed=2 * pixels, transcendentals=0)


def send(here, readings, blocks):
    rows, depth = readings.shape[0] // 2, readings.shape[1]
    parts = [part for block in blocks for part in block]
    return pl.pallas_call(
        functools.partial(send_kernel, 1.0 / math.sqrt(depth), [len(block) for block in blocks]),
        in_specs=[SMEM, VMEM] + [VMEM] * len(parts),
        out_specs=VMEM,
        out_shape=jax.ShapeDtypeStruct((len(blocks), rows, parts[0].shape[1]), BF16),
        cost_estimate=cost(blocks, rows),
        compiler_params=PARAMS,
        name="send",
    )(here, readings, *parts)


def keep(here, readings, blocks, shifts):
    rows, depth = readings.shape[0] // 2, readings.shape[1]
    parts = [part for block in blocks for part in block]
    count, width = len(blocks), parts[0].shape[1]
    return pl.pallas_call(
        functools.partial(
            keep_kernel, 1.0 / math.sqrt(depth), count, shifts, [len(block) for block in blocks]
        ),
        in_specs=[SMEM, VMEM] + [VMEM] * len(parts),
        out_specs=HBM,
        out_shape=jax.ShapeDtypeStruct((rows, 2 * count * width), BF16),
        scratch_shapes=[pltpu.VMEM((count, rows, width), BF16), pltpu.SemaphoreType.DMA((count,))],
        cost_estimate=cost(blocks, rows),
        compiler_params=PARAMS,
        name="keep",
    )(here, readings, *parts)


def place(here, pieces, shifts, whole):
    return pl.pallas_call(
        functools.partial(place_kernel, len(shifts), shifts),
        in_specs=[SMEM] + [HBM] * (len(pieces) + 1),
        out_specs=HBM,
        out_shape=jax.ShapeDtypeStruct(whole.shape, BF16),
        scratch_shapes=[pltpu.SemaphoreType.DMA((len(shifts),))],
        input_output_aliases={len(pieces) + 1: 0},
        compiler_params=PARAMS,
        name="place",
    )(here, *pieces, whole)


def ring(value, shift):
    size = lax.axis_size("z")
    return lax.ppermute(value, "z", [(i, (i + shift) % size) for i in range(size)])


def body(temps, sensors):
    tiers, snaps, width = temps.shape
    depth = tiers * snaps
    n_side, n_lists, n_plane, devices = (lax.axis_size(a) for a in (SIDE, LISTS, PLANE, AXES))
    group = sensors.shape[1] // n_lists
    z, xl = lax.axis_index("z"), lax.axis_index("xl")

    pixels = temps.reshape(depth, width)
    up, down = [pixels, ring(pixels, 1)], [pixels]

    def go_on(blocks, shift, ready):
        block, _ = lax.optimization_barrier((blocks[-1], ready))
        blocks.append(ring(block, shift))

    first = lax.axis_index(AXES) * width
    side = lax.axis_index("xh") * 32 + lax.axis_index("core") * 16 + xl
    def listed(number):
        return compact(jnp.stack([first, number * SLOTS]), sensors, temps, n_lists)

    def exchanged(lists):
        return lax.all_to_all(lists, LISTS, 0, 0, tiled=True)

    chosen = lax.dynamic_slice_in_dim(sensors, lax.axis_index(LISTS) * group, group, axis=1)

    def part_of(number, lists):
        return expand(jnp.stack([side, number * SLOTS]), chosen, lists, width)

    lists = listed(jnp.int32(0))
    go_on(down, -1, lists)
    seen, _ = lax.optimization_barrier((sensors, lists))
    rounds = pl.cdiv(longest(seen, group, devices, width), SLOTS)
    _, part = lax.while_loop(
        lambda state: state[0] < rounds,
        lambda state: (state[0] + 1, state[1] + part_of(state[0], exchanged(listed(state[0])))),
        (jnp.int32(1), part_of(jnp.int32(0), exchanged(lists))),
    )
    go_on(up, 1, part)
    go_on(down, -1, part)
    part = lax.all_to_all(part.reshape(n_side, group // n_side, depth), SIDE, 0, 0, tiled=True)
    part = part.astype(F32).sum(axis=0).astype(BF16)
    go_on(up, 1, part)
    go_on(down, -1, part)
    copies = jnp.broadcast_to(part[None], (n_plane, *part.shape))
    readings = lax.all_to_all(copies, PLANE, 0, 0, tiled=True).reshape(-1, depth)

    here = jnp.stack([z, xl])

    def swapped(sent):
        return lax.ppermute(sent, "xl", [(0, 1), (1, 0)])

    sent = send(here, readings, [(block,) for block in (pixels, up[1], down[1], up[2], down[2])])
    above, below, _ = lax.optimization_barrier((up[3], down[3], sent))
    middle = depth // 2
    far = (ring(above[:middle], 1), ring(below[middle:], -1))
    blocks = [(block,) for block in (*up[:2], down[1], up[2], down[2], up[3], down[3])] + [far]
    shifts = [0, -1, 1, -2, 2, -3, 3, 4]
    pieces = [swapped(sent)]
    pieces += [swapped(send(here, readings, blocks[low:high])) for low, high in ((5, 7), (7, 8))]
    return place(here, pieces, shifts, keep(here, readings, blocks, shifts))


def solution(mesh):
    torus = Mesh(mesh.devices.reshape(8, 2, 2, 8, 2), AXES)
    return jax.shard_map(
        body,
        mesh=torus,
        in_specs=(P(None, None, AXES), P()),
        out_specs=P(("z", "xl"), ("y", "xh", "core")),
        check_vma=False,
    )
```

```python
import functools
import math

import jax
import jax.numpy as jnp
from jax import lax
from jax.experimental import pallas as pl
from jax.experimental.pallas import tpu as pltpu
from jax.sharding import Mesh
from jax.sharding import PartitionSpec as P

AXES = ("y", "xh", "core", "z", "xl")
LISTS = ("z", "y")
SIDE = ("xh", "xl", "core")
PLANE = ("y", "xh", "xl", "core")
SLOTS = 8
F32, BF16 = jnp.float32, jnp.bfloat16
PARAMS = pltpu.CompilerParams(vmem_limit_bytes=16 * 2**20)
NT = (((1,), (1,)), ((), ()))
VMEM = pl.BlockSpec(memory_space=pltpu.VMEM)
SMEM = pl.BlockSpec(memory_space=pltpu.SMEM)
HBM = pl.BlockSpec(memory_space=pl.ANY)


def matmul(a, b, dims=(((1,), (0,)), ((), ()))):
    return lax.dot_general(a, b, dims, preferred_element_type=F32)


def ones(mask):
    return mask.astype(F32).astype(BF16)


def compact_kernel(scalar_ref, sensors_ref, temps_ref, out_ref):
    tiers, snaps, width = temps_ref.shape
    count, rows = sensors_ref.shape[1], out_ref.shape[0]
    span = 256
    group = count * SLOTS // rows
    first, start = scalar_ref[0], scalar_ref[1]
    before = lax.broadcasted_iota(jnp.int32, (span, span), 0)
    after = lax.broadcasted_iota(jnp.int32, (span, span), 1)
    together = before // group == after // group
    ahead, together = ones(together & (before < after)), ones(together)
    lower = ones(
        lax.broadcasted_iota(jnp.int32, (tiers, tiers), 0)
        > lax.broadcasted_iota(jnp.int32, (tiers, tiers), 1)
    )
    made = span * SLOTS // group
    row_ids = lax.broadcasted_iota(jnp.int32, (made, span), 0)
    tier_ids = lax.broadcasted_iota(jnp.int32, (tiers, span), 0)
    list_ids = lax.broadcasted_iota(jnp.int32, (tiers, span), 1) // group
    spots = []
    for low in range(0, count, span):
        offset = sensors_ref[:, low : low + span] - first
        mine = (offset >= 0) & (offset < width)
        held = ones(mine)
        slot = matmul(held, ahead) + matmul(matmul(lower, held).astype(BF16), together)
        slot = slot.astype(jnp.int32) - start
        slot = jnp.where(mine & (slot >= 0) & (slot < SLOTS), slot + list_ids * SLOTS, -1)
        spot = (offset + tier_ids * width + 1).astype(F32)
        found = jnp.zeros((made, span), F32)
        for tier in range(tiers):
            row = slice(tier, tier + 1)
            found = found + jnp.where(slot[row] == row_ids, spot[row], 0.0)
        spots.append(found.sum(axis=1, keepdims=True))
    spots = jnp.concatenate(spots, axis=0).astype(jnp.int32) - 1
    lanes = lax.broadcasted_iota(jnp.int32, (rows, width), 1)
    total = jnp.zeros((rows, snaps), F32)
    for tier in range(tiers):
        total = total + matmul(ones(spots - tier * width == lanes), temps_ref[tier], NT)
    out_ref[...] = jnp.concatenate([total, jnp.zeros_like(total)], axis=1).astype(BF16)


def compact(scalars, sensors, temps, lists):
    snaps = temps.shape[1]
    return pl.pallas_call(
        compact_kernel,
        in_specs=[SMEM, VMEM, VMEM],
        out_specs=VMEM,
        out_shape=jax.ShapeDtypeStruct((lists * SLOTS, 2 * snaps), BF16),
        compiler_params=PARAMS,
        name="compact",
    )(scalars, sensors, temps).reshape(lists, SLOTS, 2 * snaps)


def expand_kernel(shift, scalar_ref, rows_ref, columns_ref, lists_ref, out_ref):
    tiers, group = rows_ref.shape
    n_lists, slots, wide = lists_ref.shape
    side, start = scalar_ref[0], scalar_ref[1]
    rows, owners = rows_ref[...] >> shift, columns_ref[...] >> shift
    later = lax.broadcasted_iota(jnp.int32, (group, group), 0) > lax.broadcasted_iota(
        jnp.int32, (group, group), 1
    )
    lists = lists_ref[...].reshape(n_lists * slots, wide)
    lanes = lax.broadcasted_iota(jnp.int32, (group, n_lists * slots), 1)
    found = []
    for tier in range(tiers):
        owner = owners[:, tier : tier + 1]
        same = [(owner == rows[t : t + 1]).astype(F32) for t in range(tier + 1)]
        same[-1] = jnp.where(later, same[-1], 0.0)
        slot = sum(same[1:], same[0]).sum(axis=1, keepdims=True).astype(jnp.int32) - start
        sender = (owner >> 1 & 7) * 8 + (owner >> 6)
        there = (owner & 49 == side) & (slot >= 0) & (slot < slots)
        spot = jnp.where(there, sender * slots + slot, -1)
        found.append(matmul(ones(spot == lanes), lists)[:, : wide // 2])
    for tier in range(0, tiers, 2):
        pair = jnp.concatenate(found[tier : tier + 2], axis=1)
        out_ref[:, tier * wide // 2 : (tier + 2) * wide // 2] = pair.astype(BF16)


def expand(scalars, chosen, lists, width):
    tiers, group = chosen.shape
    return pl.pallas_call(
        functools.partial(expand_kernel, width.bit_length() - 1),
        in_specs=[SMEM, VMEM, VMEM, VMEM],
        out_specs=VMEM,
        out_shape=jax.ShapeDtypeStruct((group, tiers * lists.shape[2] // 2), BF16),
        compiler_params=PARAMS,
        name="expand",
    )(scalars, chosen, chosen.T, lists)


def longest_kernel(group, devices, shift, sensors_ref, out_ref):
    tiers, count = sensors_ref.shape
    span, low = 256, 16
    lists = span // group
    high_ids = lax.broadcasted_iota(jnp.int32, (devices // low, span), 0)
    low_ids = lax.broadcasted_iota(jnp.int32, (low * lists, span), 0)
    list_ids = lax.broadcasted_iota(jnp.int32, (1, span), 1) // group
    most = jnp.zeros((devices // low, low * lists), F32)
    for at in range(0, count, span):
        owner = sensors_ref[:, at : at + span] >> shift
        total = jnp.zeros_like(most)
        for tier in range(tiers):
            row = owner[tier : tier + 1]
            lows = (row & low - 1) + list_ids * low
            total = total + matmul(ones(row >> 4 == high_ids), ones(lows == low_ids), NT)
        most = jnp.maximum(most, total)
    out_ref[0, 0] = jnp.max(most).astype(jnp.int32)


def longest(sensors, group, devices, width):
    return pl.pallas_call(
        functools.partial(longest_kernel, group, devices, width.bit_length() - 1),
        in_specs=[VMEM],
        out_specs=SMEM,
        out_shape=jax.ShapeDtypeStruct((1, 1), jnp.int32),
        cost_estimate=pl.CostEstimate(
            flops=100 * sensors.size * devices, bytes_accessed=4 * sensors.size, transcendentals=0
        ),
        compiler_params=PARAMS,
        name="longest",
    )(sensors)[0, 0]


def correlation(scale, readings, block):
    depth = readings.shape[1] // len(block)
    parts = [
        matmul(readings[:, i * depth : (i + 1) * depth], part[...]) for i, part in enumerate(block)
    ]
    return (sum(parts[1:], parts[0]) * scale).astype(BF16)


def half_of(readings_ref, side):
    rows = readings_ref.shape[0] // 2
    return readings_ref[pl.ds(pl.multiple_of(side * rows, rows), rows)]


def grouped(refs, sizes):
    refs = iter(refs)
    return [[next(refs) for _ in range(size)] for size in sizes]


def send_kernel(scale, sizes, scalar_ref, readings_ref, *rest):
    readings = half_of(readings_ref, 1 - scalar_ref[1])
    for spot, block in enumerate(grouped(rest[:-1], sizes)):
        rest[-1][spot] = correlation(scale, readings, block)


def keep_kernel(scale, n_z, shifts, sizes, scalar_ref, readings_ref, *rest):
    *refs, out_ref, made, stored = rest
    readings = half_of(readings_ref, scalar_ref[1])
    stores = []
    for spot, block in enumerate(grouped(refs, sizes)):
        made[spot] = correlation(scale, readings, block)
        stores.append(
            pltpu.make_async_copy(
                made.at[spot], columns(out_ref, n_z, shifts[spot], scalar_ref, 0), stored.at[spot]
            )
        )
        stores[-1].start()
    for store in stores:
        store.wait()


def columns(out_ref, n_z, shift, scalar_ref, other):
    width = out_ref.shape[1] // (2 * n_z)
    side = 1 - scalar_ref[1] if other else scalar_ref[1]
    spot = (2 * lax.rem(scalar_ref[0] + shift + n_z, n_z) + side) * width
    return out_ref.at[:, pl.ds(pl.multiple_of(spot, width), width)]


def place_kernel(n_z, shifts, scalar_ref, *rest):
    *pieces, _, out_ref, done = rest
    stores = []
    for piece in pieces:
        for i in range(piece.shape[0]):
            spot = len(stores)
            stores.append(
                pltpu.make_async_copy(
                    piece.at[i], columns(out_ref, n_z, shifts[spot], scalar_ref, 1), done.at[spot]
                )
            )
            stores[-1].start()
    for store in stores:
        store.wait()


def cost(blocks, rows):
    pixels = sum(part.size for block in blocks for part in block)
    return pl.CostEstimate(flops=2 * rows * pixels, bytes_accessed=2 * pixels, transcendentals=0)


def send(here, readings, blocks):
    rows, depth = readings.shape[0] // 2, readings.shape[1]
    parts = [part for block in blocks for part in block]
    return pl.pallas_call(
        functools.partial(send_kernel, 1.0 / math.sqrt(depth), [len(block) for block in blocks]),
        in_specs=[SMEM, VMEM] + [VMEM] * len(parts),
        out_specs=VMEM,
        out_shape=jax.ShapeDtypeStruct((len(blocks), rows, parts[0].shape[1]), BF16),
        cost_estimate=cost(blocks, rows),
        compiler_params=PARAMS,
        name="send",
    )(here, readings, *parts)


def keep(here, readings, blocks, shifts):
    rows, depth = readings.shape[0] // 2, readings.shape[1]
    parts = [part for block in blocks for part in block]
    count, width = len(blocks), parts[0].shape[1]
    return pl.pallas_call(
        functools.partial(
            keep_kernel, 1.0 / math.sqrt(depth), count, shifts, [len(block) for block in blocks]
        ),
        in_specs=[SMEM, VMEM] + [VMEM] * len(parts),
        out_specs=HBM,
        out_shape=jax.ShapeDtypeStruct((rows, 2 * count * width), BF16),
        scratch_shapes=[pltpu.VMEM((count, rows, width), BF16), pltpu.SemaphoreType.DMA((count,))],
        cost_estimate=cost(blocks, rows),
        compiler_params=PARAMS,
        name="keep",
    )(here, readings, *parts)


def place(here, pieces, shifts, whole):
    return pl.pallas_call(
        functools.partial(
            place_kernel, whole.shape[1] // (2 * pieces[0].shape[2]), shifts
        ),
        in_specs=[SMEM] + [HBM] * (len(pieces) + 1),
        out_specs=HBM,
        out_shape=jax.ShapeDtypeStruct(whole.shape, BF16),
        scratch_shapes=[pltpu.SemaphoreType.DMA((len(shifts),))],
        input_output_aliases={len(pieces) + 1: 0},
        compiler_params=PARAMS,
        name="place",
    )(here, *pieces, whole)


def ring(value, shift):
    size = lax.axis_size("z")
    return lax.ppermute(value, "z", [(i, (i + shift) % size) for i in range(size)])


def body(temps, sensors):
    tiers, snaps, width = temps.shape
    depth = tiers * snaps
    n_side, n_lists, n_plane, devices = (lax.axis_size(a) for a in (SIDE, LISTS, PLANE, AXES))
    group = sensors.shape[1] // n_lists
    z, xl = lax.axis_index("z"), lax.axis_index("xl")

    pixels = temps.reshape(depth, width)
    up, down = [pixels, ring(pixels, 1)], [pixels, ring(pixels, -1)]

    def go_on(blocks, shift, ready):
        block, _ = lax.optimization_barrier((blocks[-1], ready))
        blocks.append(ring(block, shift))

    first = lax.axis_index(AXES) * width
    side = lax.axis_index("xh") * 32 + lax.axis_index("core") * 16 + xl
    def listed(number):
        return compact(jnp.stack([first, number * SLOTS]), sensors, temps, n_lists)

    def exchanged(lists):
        return lax.all_to_all(lists, LISTS, 0, 0, tiled=True)

    chosen = lax.dynamic_slice_in_dim(sensors, lax.axis_index(LISTS) * group, group, axis=1)

    def part_of(number, lists):
        return expand(jnp.stack([side, number * SLOTS]), chosen, lists, width)

    lists = listed(jnp.int32(0))
    seen, _ = lax.optimization_barrier((sensors, lists))
    rounds = pl.cdiv(longest(seen, group, devices, width), SLOTS)
    _, part = lax.while_loop(
        lambda state: state[0] < rounds,
        lambda state: (state[0] + 1, state[1] + part_of(state[0], exchanged(listed(state[0])))),
        (jnp.int32(1), part_of(jnp.int32(0), exchanged(lists))),
    )
    go_on(up, 1, part)
    go_on(down, -1, part)
    part = lax.all_to_all(part.reshape(n_side, group // n_side, depth), SIDE, 0, 0, tiled=True)
    part = part.astype(F32).sum(axis=0).astype(BF16)
    go_on(up, 1, part)
    go_on(down, -1, part)
    copies = jnp.broadcast_to(part[None], (n_plane, *part.shape))
    readings = lax.all_to_all(copies, PLANE, 0, 0, tiled=True).reshape(-1, depth)

    here = jnp.stack([z, xl])

    def swapped(sent):
        return lax.ppermute(sent, "xl", [(0, 1), (1, 0)])

    sent = send(here, readings, [(block,) for block in (pixels, up[1], down[1], up[2], down[2])])
    above, below, _ = lax.optimization_barrier((up[3], down[3], sent))
    middle = depth // 2
    far = (ring(above[:middle], 1), ring(below[middle:], -1))
    blocks = [(block,) for block in (*up[:2], down[1], up[2], down[2], up[3], down[3])] + [far]
    shifts = [0, -1, 1, -2, 2, -3, 3, 4]
    pieces = [swapped(sent)]
    pieces += [swapped(send(here, readings, blocks[low:high])) for low, high in ((5, 7), (7, 8))]
    whole = place(here, pieces[:2], shifts[:7], keep(here, readings, blocks, shifts))
    return place(here, pieces[2:], shifts[7:], whole)


def solution(mesh):
    torus = Mesh(mesh.devices.reshape(8, 2, 2, 8, 2), AXES)
    return jax.shard_map(
        body,
        mesh=torus,
        in_specs=(P(None, None, AXES), P()),
        out_specs=P(("z", "xl"), ("y", "xh", "core")),
        check_vma=False,
    )
```
